512 devices in a mesh: expert: 128 (over y, z, core), rep: 4 (over x).
Axes of the slice: x: 4, y: 8, z: 8, core: 2. Of those that a mesh axis runs over, the one named last changes fastest.
Arguments:
- tokens: bfloat16 [16384, 1024], P('expert', 'rep'), may hold values from -6 to 6
- cotangent: bfloat16 [16384, 1024], P('expert', 'rep'), may hold values from -1.796875 to 1.796875
- expert_ids: int32 [16384, 2], P('expert'), may hold values from 0 to 127, all different within a row; in each aligned block of 128 rows (0 to 127, 128 to 255, ...) at most 4 rows name the same one
- gate_values: float32 [16384, 2], P('expert'), may hold values from 0.1 to 0.9
- inner_weight: bfloat16 [128, 1024, 4096], P('expert', None, 'rep'), may hold values from -0.1875 to 0.1875
- outer_weight: bfloat16 [128, 4096, 1024], P('expert', 'rep'), may hold values from -0.09375 to 0.09375
Outputs:
- output: bfloat16 [16384, 1024], P('expert', 'rep')
- input_grads: bfloat16 [16384, 1024], P('expert', 'rep')
- gate_grads: float32 [16384, 2], P('expert')
The draws below stay inside these ranges and needn't reach their ends.
Inputs may be any that keep to these rules, and one draw needn't show every extreme that they name: `expert_ids`: each token names 2 different experts. Among the 128 tokens of one block no expert is named more than 4 times, a bound that some block reaches.
All inputs are finite; a program needn't handle non-finite values.
Results may differ from the reference program's by a relative error of at most 0.012.
Values may be sent and summed in bfloat16 or wider, within the bound.
No kernel may reach another device: no remote copies, remote signals or barrier semaphores. Data moves between devices by JAX's collectives and lax.ppermute only.
A program may use at most 64 MiB of HBM per device.

```python
import math
import jax
import jax.numpy as jnp
import numpy as np
from jax import lax

D = 1024
EXPERTS = 128
TOP = 2
FF_W = 4096
TOK = 128
CAP = 4
TOKENS = 16384
N_REP = 4


def levels(stream_key, extent, pieces, low, top_value):
    loudness = 1.0
    for dim, shards_of in pieces:
        draws = jax.random.uniform(jax.random.fold_in(jax.random.fold_in(stream_key, 6), dim), (shards_of,), jnp.float32, low / len(pieces), top_value / len(pieces))
        loudness = loudness * jnp.repeat(jnp.exp(draws), extent[dim] // shards_of).reshape((-1,) + (1,) * (len(extent) - 1 - dim))
    return loudness


def assign_block(stream_key, own, number, rows, number_of, top, reach, skew):
    order = jax.random.permutation(stream_key, number_of)
    heavy_load, usual = portions_of(number_of, rows * top, reach, skew, True), portions_of(number_of, rows * top, reach, skew, False)
    places = jnp.arange(number_of)

    def named(lengths, rotation):
        used = int((lengths > 0).sum())
        fixed = max(1, used // 4)
        passed = fixed + (places - fixed + rotation * (used - fixed)) % max(1, number_of - fixed)
        return jnp.zeros((number_of,), jnp.int32).at[order[jnp.where(places < fixed, places, passed)]].set(jnp.asarray(lengths, jnp.int32))

    lengths = jnp.where(number % 4 == 0, named(heavy_load, number // 4), named(usual, number - number // 4 - 1))
    mixed = jax.random.permutation(jax.random.fold_in(own, 3), number_of)
    giver, receiver = mixed[0:number_of // 2 * 2:2], mixed[1:number_of // 2 * 2:2]
    room = jnp.minimum(lengths[giver] - 1, reach - lengths[receiver]) // 2
    room = jnp.where((giver == order[0]) | (receiver == order[0]) | (lengths[receiver] == 0), 0, jnp.maximum(room, 0))
    passed = jax.random.randint(jax.random.fold_in(own, 4), (number_of // 2,), 0, 1 << 20) % (room + 1)
    lengths = lengths.at[giver].add(-passed).at[receiver].add(passed)
    members = jnp.searchsorted(jnp.cumsum(lengths), jnp.arange(rows * top), side="right").astype(jnp.int32)
    grid = members.reshape(top, rows).T
    grid = grid[jax.random.permutation(jax.random.fold_in(own, 1), rows)]
    rotation = jax.random.randint(jax.random.fold_in(own, 2), (rows, 1), 0, top)
    return jnp.take_along_axis(grid, (jnp.arange(top)[None, :] + rotation) % top, axis=1)


def portions_of(number_of, total, limit, slope, full):
    weights = [(1 << 20) // math.isqrt(standing ** slope) + 1 for standing in range(1, number_of + 1)]
    largest = limit if full else min(limit, max(-(-total // number_of), total * weights[0] // sum(weights)))
    least = 1 if total - largest >= number_of - 1 else 0
    counts, rest = [largest] + [least] * (number_of - 1), total - largest - least * (number_of - 1)
    while rest > 0:
        free = [i for i in range(1, number_of) if counts[i] < largest] or [i for i in range(1, number_of) if counts[i] < limit]
        mass, remaining = sum([weights[i] for i in free]), rest
        for i in free:
            more = min(limit - counts[i], max(1, remaining * weights[i] // mass), rest)
            counts[i] = counts[i] + more
            rest = rest - more
    return np.array(counts)


def normal_values(rng, extent, spread, limit, shards=(), kind=jnp.bfloat16):
    level = levels(rng, extent, shards, -0.22, 0.18) if shards else 1.0
    entries = jax.random.normal(rng, extent, jnp.float32) * spread * level
    return jnp.minimum(jnp.maximum(entries, -limit), limit).astype(kind)


def setup_inputs(seed: int = 0) -> dict:
    splits = jax.random.split(jax.random.key(seed), 7)
    tokens = normal_values(splits[0], (TOKENS, D), 1.0, 6.0, ((0, 128), (1, 4)))
    cotangent = normal_values(splits[1], (TOKENS, D), 0.3, 1.796875, ((0, 128), (1, 4)))
    expert_ids_keys = jax.random.split(jax.random.fold_in(splits[2], 1), TOKENS // TOK)
    expert_ids_turns = jax.random.permutation(jax.random.fold_in(splits[2], 3), TOKENS // TOK)
    expert_ids = jax.vmap(lambda own, number: assign_block(jax.random.fold_in(splits[2], 2), own, number, TOK, EXPERTS, TOP, CAP, 2))(expert_ids_keys, expert_ids_turns).reshape((TOKENS, TOP))
    gate_values = jnp.clip(0.1 + 0.79999997 * jax.random.uniform(splits[3], (TOKENS, TOP), jnp.float32) ** levels(splits[3], (TOKENS, TOP), ((0, 128),), -0.2, 0.2), 0.1, 0.9)
    inner_weight = normal_values(splits[4], (EXPERTS, D, FF_W), D ** -0.5, 0.1875, ((0, 128), (2, 4)))
    outer_weight = normal_values(splits[5], (EXPERTS, FF_W, D), FF_W ** -0.5, 0.09375, ((0, 128), (1, 4)))
    return dict(tokens=tokens, cotangent=cotangent, expert_ids=expert_ids, gate_values=gate_values, inner_weight=inner_weight, outer_weight=outer_weight)


SQRT_TWO_PI = 0.7978845608028654
CUBIC = 0.044715


def gelu_pair(preact):
    argument = SQRT_TWO_PI * (preact + CUBIC * preact * preact * preact)
    tangent = jnp.tanh(argument)
    result = 0.5 * preact * (1.0 + tangent)
    derivative = 0.5 * (1.0 + tangent) + 0.5 * preact * (1.0 - tangent * tangent) * SQRT_TWO_PI * (1.0 + 3.0 * CUBIC * preact * preact)
    return result, derivative


def grouped_out(hidden, outer):
    group = FF_W // N_REP
    total = jnp.zeros((hidden.shape[0], outer.shape[1]), jnp.float32)
    for part in range(N_REP):
        piece = jnp.dot(hidden[:, part * group:(part + 1) * group], outer[part * group:(part + 1) * group, :], preferred_element_type=jnp.float32)
        total = total + piece.astype(jnp.bfloat16).astype(jnp.float32)
    return total.astype(jnp.bfloat16)


def grouped_in(back_pre, inner):
    group = FF_W // N_REP
    total = jnp.zeros((back_pre.shape[0], inner.shape[0]), jnp.float32)
    for part in range(N_REP):
        piece = lax.dot_general(back_pre[:, part * group:(part + 1) * group], inner[:, part * group:(part + 1) * group], (((1,), (1,)), ((), ())), preferred_element_type=jnp.float32)
        total = total + piece.astype(jnp.bfloat16).astype(jnp.float32)
    return total.astype(jnp.bfloat16)


def reference(tokens, cotangent, expert_ids, gate_values, inner_weight, outer_weight):
    blocks = TOKENS // TOK
    assigns = TOK * TOP
    block_ids = expert_ids.reshape(blocks, assigns).astype(jnp.int32)
    matches = (block_ids[:, :, None] == jnp.arange(EXPERTS, dtype=jnp.int32)[None, None, :]).astype(jnp.int32)
    ranked = jnp.sum((jnp.cumsum(matches, axis=1) - 1) * matches, axis=2).astype(jnp.int32)
    position = (block_ids * blocks + jnp.arange(blocks, dtype=jnp.int32)[:, None]) * CAP + ranked
    owners = jnp.full((EXPERTS * blocks * CAP,), -1, dtype=jnp.int32)
    owners = owners.at[position.reshape(-1)].set(jnp.arange(TOKENS * TOP, dtype=jnp.int32))
    owners = owners.reshape(EXPERTS, blocks * CAP)
    flat_gates = gate_values.reshape(-1)

    def per_expert(carry, inputs):
        out_store, in_store = carry
        owner_row, inner, outer = inputs
        valid = owner_row >= 0
        safe = jnp.where(valid, owner_row, 0).astype(jnp.int32)
        token_index = (safe // TOP).astype(jnp.int32)
        expert_rows = jnp.where(valid[:, None], tokens[token_index], jnp.zeros((), tokens.dtype))
        gate_here = jnp.where(valid, flat_gates[safe], jnp.zeros((), flat_gates.dtype))
        expert_grads = (gate_here[:, None] * cotangent[token_index].astype(jnp.float32)).astype(jnp.bfloat16)
        preact = jnp.dot(expert_rows, inner, preferred_element_type=jnp.float32)
        result, derivative = gelu_pair(preact)
        hidden = result.astype(jnp.bfloat16)
        expert_out = grouped_out(hidden, outer)
        back_hidden = lax.dot_general(expert_grads, outer, (((1,), (1,)), ((), ())), preferred_element_type=jnp.float32)
        back_pre = (back_hidden * derivative).astype(jnp.bfloat16)
        slot_input = grouped_in(back_pre, inner)
        target = jnp.where(valid, owner_row, TOKENS * TOP).astype(jnp.int32)
        out_store = out_store.at[target].set(expert_out, mode="drop")
        in_store = in_store.at[target].set(slot_input, mode="drop")
        return (out_store, in_store), None

    start_store = (jnp.zeros((TOKENS * TOP, D), jnp.bfloat16), jnp.zeros((TOKENS * TOP, D), jnp.bfloat16))
    (out_store, in_store), unused = lax.scan(per_expert, start_store, (owners, inner_weight, outer_weight))
    out_store = out_store.reshape(TOKENS, TOP, D)
    in_store = in_store.reshape(TOKENS, TOP, D)
    cot_wide = cotangent.astype(jnp.float32)
    combined = jnp.zeros((TOKENS, D), jnp.float32)
    in_total = jnp.zeros((TOKENS, D), jnp.float32)
    columns = []
    for member in range(TOP):
        picked = out_store[:, member, :].astype(jnp.float32)
        combined = combined + gate_values[:, member:member + 1] * picked
        columns.append(jnp.sum(cot_wide * picked, axis=1))
        in_total = in_total + in_store[:, member, :].astype(jnp.float32)
    output = combined.astype(jnp.bfloat16)
    input_grads = in_total.astype(jnp.bfloat16)
    gate_grads = jnp.stack(columns, axis=1)
    return output, input_grads, gate_grads
```

```python
import jax
import jax.numpy as jnp
from jax import lax
from jax.experimental import pallas as pl
from jax.experimental.pallas import tpu as pltpu
from jax.sharding import PartitionSpec as P

TOP = 2
EXTRA = 16

SQRT_TWO_PI = 0.7978845608028654
CUBIC = 0.044715

PARAMS = pltpu.CompilerParams(vmem_limit_bytes=24 * 1024 * 1024)


def iota(shape, dim):
    return lax.broadcasted_iota(jnp.int32, shape, dim)


def slot_positions(ids, experts, capacity):
    rows = ids.shape[1]
    of_expert = iota((experts, rows), 0)
    named = [of_expert == ids[k : k + 1, :] for k in range(TOP)]
    both = sum(jnp.where(m, 1.0, 0.0) for m in named)
    earlier = jnp.where(iota((rows, rows), 0) < iota((rows, rows), 1), 1.0, 0.0)
    before = jnp.dot(
        both.astype(jnp.bfloat16), earlier.astype(jnp.bfloat16), preferred_element_type=jnp.float32
    )
    ranks = [jnp.sum(jnp.where(m, before, 0.0), axis=0, keepdims=True) for m in named]
    return [ids[k : k + 1, :] * capacity + ranks[k].astype(jnp.int32) for k in range(TOP)]


def column_of(row):
    n = row.shape[1]
    eye = iota((n, n), 0) == iota((n, n), 1)
    return jnp.sum(jnp.where(eye, row, jnp.zeros_like(row)), axis=1, keepdims=True)


def row_of(column):
    n = column.shape[0]
    eye = iota((n, n), 0) == iota((n, n), 1)
    return jnp.sum(jnp.where(eye, column, jnp.zeros_like(column)), axis=0, keepdims=True)


def pack_kernel(
    experts, capacity, ids_in, token_in, cot_in, out_ref, ids_ref, token_ref, cot_ref, sems
):
    copies = [
        pltpu.make_async_copy(src, dst, sems.at[i])
        for i, (src, dst) in enumerate(
            ((ids_in, ids_ref), (token_in, token_ref), (cot_in, cot_ref))
        )
    ]
    for copy in copies:
        copy.start()
    copies[0].wait()
    quarter = token_ref.shape[1]
    positions = slot_positions(ids_ref[...], experts, capacity)
    slot = iota((experts * capacity, token_ref.shape[0]), 0)
    hit = slot == positions[0]
    for k in range(1, TOP):
        hit = hit | (slot == positions[k])
    table = jnp.where(hit, 1.0, 0.0).astype(jnp.bfloat16)
    for part, ref in enumerate((token_ref, cot_ref)):
        copies[1 + part].wait()
        out_ref[:, part * quarter : (part + 1) * quarter] = jnp.dot(
            table, ref[...], preferred_element_type=jnp.float32
        ).astype(jnp.bfloat16)


def fetch(source, target, sem):
    copy = pltpu.make_async_copy(source, target, sem)
    copy.start()
    return copy


def forward_kernel(
    rows_ref,
    inner_in,
    outer_in,
    outs_out,
    hidden_out,
    slope_out,
    inner_ref,
    outer_ref,
    outs_ref,
    hidden_ref,
    slope_ref,
    pre_ref,
    sems,
):
    parts, slots, quarter = rows_ref.shape
    piece = [slice(q * quarter, (q + 1) * quarter) for q in range(parts)]
    inner_copies = [
        fetch(inner_in.at[piece[q], :], inner_ref.at[piece[q], :], sems.at[q]) for q in range(parts)
    ]
    outer_copy = fetch(outer_in, outer_ref, sems.at[parts])
    acc = None
    for q in range(parts):
        inner_copies[q].wait()
        term = jnp.dot(rows_ref[q], inner_ref[piece[q], :], preferred_element_type=jnp.float32)
        acc = term if acc is None else acc + term
    pre_ref[...] = acc
    step = 16

    def activate(i, carry):
        at = pl.ds(pl.multiple_of(i * step, step), step)
        u = pre_ref[at, :]
        tangent = jnp.tanh(SQRT_TWO_PI * (u + CUBIC * u * u * u))
        hidden_ref[at, :] = (0.5 * u * (1.0 + tangent)).astype(jnp.bfloat16)
        slope_ref[at, :] = (
            0.5 * (1.0 + tangent)
            + 0.5
            * u
            * (1.0 - tangent * tangent)
            * SQRT_TWO_PI
            * (1.0 + 3.0 * CUBIC * u * u)
        )
        return carry

    lax.fori_loop(0, slots // step, activate, 0)
    saves = [
        fetch(hidden_ref, hidden_out, sems.at[parts + 1]),
        fetch(slope_ref, slope_out, sems.at[parts + 2]),
    ]
    outer_copy.wait()
    for q in range(parts):
        outs_ref[q] = jnp.dot(
            hidden_ref[...], outer_ref[:, piece[q]], preferred_element_type=jnp.float32
        ).astype(jnp.bfloat16)
        saves.append(fetch(outs_ref.at[q], outs_out.at[q], sems.at[parts + 3 + q]))
    for copy in saves:
        copy.wait()


def backward_kernel(parts, me_ref, *refs):
    cot_ins = refs[:parts]
    hidden_in, slope_in, inner_in, outer_in, in_ref = refs[parts : parts + 5]
    (cot_ref, hidden_ref, slope_ref, inner_ref, outer_ref) = refs[parts + 5 : parts + 10]
    back_ref, grad_ref, pre_ref, sems = refs[parts + 10 :]
    slots, quarter = cot_ref.shape[1:]
    width = back_ref.shape[1]
    across = (((1,), (1,)), ((), ()))
    outer_copy = fetch(outer_in, outer_ref, sems.at[parts])
    cot_copies = [fetch(cot_ins[q], cot_ref.at[q], sems.at[q]) for q in range(parts)]
    later = [
        fetch(source, target, sems.at[parts + 1 + i])
        for i, (source, target) in enumerate(
            ((slope_in, slope_ref), (hidden_in, hidden_ref), (inner_in, inner_ref))
        )
    ]
    outer_copy.wait()
    acc = None
    for shift in range(parts):
        source = lax.rem(me_ref[0] + parts - shift, parts)
        columns = pl.ds(pl.multiple_of(source * quarter, quarter), quarter)
        cot_copies[shift].wait()
        term = lax.dot_general(
            cot_ref[shift], outer_ref[:, columns], across, preferred_element_type=jnp.float32
        )
        acc = term if acc is None else acc + term
    back_ref[...] = acc
    for copy in later:
        copy.wait()
    step = 16

    def activate(i, carry):
        at = pl.ds(pl.multiple_of(i * step, step), step)
        back = back_ref[at, :]
        pre_ref[at, :] = (back * slope_ref[at, :]).astype(jnp.bfloat16)
        product = back * hidden_ref[at, :].astype(jnp.float32)
        folded = product[:, :128]
        for j in range(1, width // 128):
            folded = folded + product[:, j * 128 : (j + 1) * 128]
        grad_ref[at, :] = folded
        return carry

    lax.fori_loop(0, slots // step, activate, 0)
    gate = lax.dot_general(
        jnp.ones((8, 128), jnp.float32),
        grad_ref[...],
        across,
        precision=lax.Precision.HIGHEST,
        preferred_element_type=jnp.float32,
    )[:1, :]
    high = gate.astype(jnp.bfloat16).astype(jnp.float32)
    low = gate - high
    place = iota((EXTRA, quarter), 0)
    extra = jnp.zeros((EXTRA, quarter), jnp.float32)
    for j in range(slots // quarter):
        piece = slice(j * quarter, (j + 1) * quarter)
        extra = jnp.where(place == 2 * j, high[:, piece], extra)
        extra = jnp.where(place == 2 * j + 1, low[:, piece], extra)
    for q in range(parts):
        in_ref[q, :slots, :] = lax.dot_general(
            pre_ref[...],
            inner_ref[q * quarter : (q + 1) * quarter, :],
            across,
            preferred_element_type=jnp.float32,
        ).astype(jnp.bfloat16)
        in_ref[q, slots:, :] = extra.astype(jnp.bfloat16)


def add_kernel(outs_ref, ins_ref, sum_ref):
    parts, slots, quarter = outs_ref.shape
    step = 16

    def add(i, carry):
        at = pl.ds(pl.multiple_of(i * step, step), step)
        total = outs_ref[0, at, :].astype(jnp.float32)
        other = ins_ref[0, at, :].astype(jnp.float32)
        for q in range(1, parts):
            total = total + outs_ref[q, at, :].astype(jnp.float32)
            other = other + ins_ref[q, at, :].astype(jnp.float32)
        sum_ref[at, :quarter] = total.astype(jnp.bfloat16)
        sum_ref[at, quarter : 2 * quarter] = other.astype(jnp.bfloat16)
        return carry

    lax.fori_loop(0, slots // step, add, 0)
    extra = ins_ref[0, slots:, :].astype(jnp.float32)
    for q in range(1, parts):
        extra = extra + ins_ref[q, slots:, :].astype(jnp.float32)
    lane = iota((128, 128), 1)
    for j in range(slots // 128):
        at, lanes = divmod(j * 128, quarter)
        gate = column_of(
            extra[2 * at : 2 * at + 1, lanes : lanes + 128]
            + extra[2 * at + 1 : 2 * at + 2, lanes : lanes + 128]
        )
        high = gate.astype(jnp.bfloat16).astype(jnp.float32)
        low = gate - high
        sum_ref[j * 128 : (j + 1) * 128, 2 * quarter :] = jnp.where(
            lane == 0, high, jnp.where(lane == 1, low, 0.0)
        ).astype(jnp.bfloat16)


def table_kernel(experts, capacity, ids_ref, table_ref):
    rows = ids_ref.shape[1]
    positions = slot_positions(ids_ref[...], experts, capacity)
    slot = iota((rows, experts * capacity), 1)
    for k in range(TOP):
        hit = slot == column_of(positions[k])
        table_ref[k * rows : (k + 1) * rows, :] = jnp.where(hit, 1.0, 0.0).astype(jnp.bfloat16)


def combine_kernel(table_ref, gates_ref, back_ref, out_ref, in_ref, gate_ref):
    rows, quarter = out_ref.shape
    total = None
    for k in range(TOP):
        picked = jnp.dot(
            table_ref[k * rows : (k + 1) * rows, :],
            back_ref[...],
            preferred_element_type=jnp.float32,
        )
        term = column_of(gates_ref[k : k + 1, :]) * picked[:, : 2 * quarter]
        total = term if total is None else total + term
        gate = picked[:, 2 * quarter : 2 * quarter + 1] + picked[:, 2 * quarter + 1 : 2 * quarter + 2]
        gate_ref[k : k + 1, :] = row_of(gate)
    out_ref[...] = total[:, :quarter].astype(jnp.bfloat16)
    in_ref[...] = total[:, quarter:].astype(jnp.bfloat16)


def to_everyone(x, axis):
    peers = lax.axis_size(axis)
    return lax.all_to_all(jnp.broadcast_to(x[None], (peers, *x.shape)), axis, 0, 0, tiled=True)


def shape_of(shape, dtype):
    return jax.ShapeDtypeStruct(shape, dtype)


def in_hbm(x):
    return pltpu.with_memory_space_constraint(x, pltpu.HBM)


def exchange(tokens, cotangent, expert_ids, gate_values, inner_weight, outer_weight):
    rows, quarter = tokens.shape
    peers = lax.axis_size("expert")
    experts = peers * inner_weight.shape[0]
    capacity = 2 * rows * TOP // experts
    slots = experts * capacity
    parts = lax.axis_size("rep")
    inner, outer = in_hbm(inner_weight[0]), in_hbm(outer_weight[0])
    depth, width = inner.shape
    ids, gates = expert_ids.T, gate_values.T
    any_spec = pl.BlockSpec(memory_space=pltpu.HBM)
    vmem_spec = pl.BlockSpec(memory_space=pltpu.VMEM)
    half, full = jnp.bfloat16, jnp.float32

    packed = pl.pallas_call(
        lambda *refs: pack_kernel(experts, capacity, *refs),
        out_shape=shape_of((slots, 2 * quarter), half),
        in_specs=[any_spec] * 3,
        scratch_shapes=[
            pltpu.VMEM(ids.shape, ids.dtype),
            pltpu.VMEM(tokens.shape, tokens.dtype),
            pltpu.VMEM(cotangent.shape, cotangent.dtype),
            pltpu.SemaphoreType.DMA((3,)),
        ],
        compiler_params=PARAMS,
        name="pack",
    )(in_hbm(ids), in_hbm(tokens), in_hbm(cotangent))
    arrived = lax.all_to_all(
        packed.reshape(peers, -1, 2 * quarter), "expert", 0, 0, tiled=True
    ).reshape(slots, 2 * quarter)
    cots = arrived[:, quarter:]
    all_rows = to_everyone(arrived[:, :quarter], "rep")
    all_cots = [cots] + [
        lax.ppermute(cots, "rep", [(i, (i + shift) % parts) for i in range(parts)])
        for shift in range(1, parts)
    ]
    table = pl.pallas_call(
        lambda *refs: table_kernel(experts, capacity, *refs),
        out_shape=shape_of((TOP * rows, slots), half),
        compiler_params=PARAMS,
        name="table",
    )(ids)
    me = lax.axis_index("rep").astype(jnp.int32).reshape(1)

    outs, hidden, slope = pl.pallas_call(
        forward_kernel,
        out_shape=(
            pltpu.HBM((parts, slots, quarter), half),
            pltpu.HBM((slots, width), half),
            pltpu.HBM((slots, width), full),
        ),
        in_specs=[vmem_spec, any_spec, any_spec],
        out_specs=(any_spec, any_spec, any_spec),
        scratch_shapes=[
            pltpu.VMEM((depth, width), half),
            pltpu.VMEM((width, depth), half),
            pltpu.VMEM((parts, slots, quarter), half),
            pltpu.VMEM((slots, width), half),
            pltpu.VMEM((slots, width), full),
            pltpu.VMEM((slots, width), full),
            pltpu.SemaphoreType.DMA((2 * parts + 3,)),
        ],
        compiler_params=PARAMS,
        name="forward",
    )(all_rows, inner, outer)
    outs = lax.all_to_all(outs, "rep", 0, 0, tiled=True)
    ins = pl.pallas_call(
        lambda *refs: backward_kernel(parts, *refs),
        out_shape=shape_of((parts, slots + EXTRA, quarter), half),
        in_specs=[pl.BlockSpec(memory_space=pltpu.SMEM)] + [any_spec] * (parts + 4),
        scratch_shapes=[
            pltpu.VMEM((parts, slots, quarter), half),
            pltpu.VMEM((slots, width), half),
            pltpu.VMEM((slots, width), full),
            pltpu.VMEM((depth, width), half),
            pltpu.VMEM((width, depth), half),
            pltpu.VMEM((slots, width), full),
            pltpu.VMEM((slots, 128), full),
            pltpu.VMEM((slots, width), half),
            pltpu.SemaphoreType.DMA((parts + 4,)),
        ],
        compiler_params=PARAMS,
        name="backward",
    )(me, *[in_hbm(x) for x in all_cots], in_hbm(hidden), in_hbm(slope), inner, outer)
    ins = lax.all_to_all(ins, "rep", 0, 0, tiled=True)
    summed = pl.pallas_call(
        add_kernel,
        out_shape=shape_of((slots, 2 * quarter + 128), half),
        compiler_params=PARAMS,
        name="add",
    )(outs, ins)
    back = lax.all_to_all(
        summed.reshape(peers, -1, 2 * quarter + 128), "expert", 0, 0, tiled=True
    ).reshape(slots, 2 * quarter + 128)
    output, input_grads, gate_grads = pl.pallas_call(
        combine_kernel,
        out_shape=(
            shape_of((rows, quarter), half),
            shape_of((rows, quarter), half),
            shape_of((TOP, rows), full),
        ),
        compiler_params=PARAMS,
        name="combine",
    )(table, gates, back)
    return output, input_grads, gate_grads.T


def solution(mesh):
    placed = (
        P("expert", "rep"),
        P("expert", "rep"),
        P("expert", None),
        P("expert", None),
        P("expert", None, "rep"),
        P("expert", "rep", None),
    )
    return jax.shard_map(
        exchange,
        mesh=mesh,
        in_specs=placed,
        out_specs=(P("expert", "rep"), P("expert", "rep"), P("expert", None)),
        check_vma=False,
    )
```

```python
import jax
import jax.numpy as jnp
from jax import lax
from jax.experimental import pallas as pl
from jax.experimental.pallas import tpu as pltpu
from jax.sharding import PartitionSpec as P

TOP = 2
EXTRA = 16

SQRT_TWO_PI = 0.7978845608028654
CUBIC = 0.044715

PARAMS = pltpu.CompilerParams(vmem_limit_bytes=24 * 1024 * 1024)


def iota(shape, dim):
    return lax.broadcasted_iota(jnp.int32, shape, dim)


def slot_positions(ids, experts, capacity):
    rows = ids.shape[1]
    of_expert = iota((experts, rows), 0)
    named = [of_expert == ids[k : k + 1, :] for k in range(TOP)]
    both = sum(jnp.where(m, 1.0, 0.0) for m in named)
    earlier = jnp.where(iota((rows, rows), 0) < iota((rows, rows), 1), 1.0, 0.0)
    before = jnp.dot(
        both.astype(jnp.bfloat16), earlier.astype(jnp.bfloat16), preferred_element_type=jnp.float32
    )
    ranks = [jnp.sum(jnp.where(m, before, 0.0), axis=0, keepdims=True) for m in named]
    return [ids[k : k + 1, :] * capacity + ranks[k].astype(jnp.int32) for k in range(TOP)]


def column_of(row):
    n = row.shape[1]
    eye = iota((n, n), 0) == iota((n, n), 1)
    return jnp.sum(jnp.where(eye, row, jnp.zeros_like(row)), axis=1, keepdims=True)


def row_of(column):
    n = column.shape[0]
    eye = iota((n, n), 0) == iota((n, n), 1)
    return jnp.sum(jnp.where(eye, column, jnp.zeros_like(column)), axis=0, keepdims=True)


def pack_kernel(
    experts, capacity, ids_in, token_in, cot_in, out_ref, ids_ref, token_ref, cot_ref, sems
):
    copies = [
        pltpu.make_async_copy(src, dst, sems.at[i])
        for i, (src, dst) in enumerate(
            ((ids_in, ids_ref), (token_in, token_ref), (cot_in, cot_ref))
        )
    ]
    for copy in copies:
        copy.start()
    copies[0].wait()
    quarter = token_ref.shape[1]
    positions = slot_positions(ids_ref[...], experts, capacity)
    slot = iota((experts * capacity, token_ref.shape[0]), 0)
    hit = slot == positions[0]
    for k in range(1, TOP):
        hit = hit | (slot == positions[k])
    table = jnp.where(hit, 1.0, 0.0).astype(jnp.bfloat16)
    for part, ref in enumerate((token_ref, cot_ref)):
        copies[1 + part].wait()
        out_ref[:, part * quarter : (part + 1) * quarter] = jnp.dot(
            table, ref[...], preferred_element_type=jnp.float32
        ).astype(jnp.bfloat16)


def fetch(source, target, sem):
    copy = pltpu.make_async_copy(source, target, sem)
    copy.start()
    return copy


def quarter_of(index, size):
    return pl.ds(pl.multiple_of(index * size, size), size)


def forward_kernel(parts, me_ref, *refs):
    row_refs = refs[:parts]
    own_in, row_refs = row_refs[0], row_refs[1:]
    inner_in, outer_in, outs_out, hidden_out, slope_out = refs[parts : parts + 5]
    (own_ref, inner_ref, outer_ref, outs_ref, hidden_ref, slope_ref, pre_ref, sems) = refs[parts + 5 :]
    slots, quarter = own_ref.shape
    piece = [slice(q * quarter, (q + 1) * quarter) for q in range(parts)]
    of = [quarter_of(lax.rem(me_ref[0] + parts - shift, parts), quarter) for shift in range(parts)]
    own_copy = fetch(own_in, own_ref, sems.at[2 * parts + 3])
    inner_copies = [
        fetch(inner_in.at[of[i], :], inner_ref.at[piece[i], :], sems.at[i]) for i in range(parts)
    ]
    outer_copy = fetch(outer_in, outer_ref, sems.at[parts])
    own_copy.wait()
    acc = None
    for i in range(parts):
        inner_copies[i].wait()
        rows = own_ref[...] if i == 0 else row_refs[i - 1][...]
        term = jnp.dot(rows, inner_ref[piece[i], :], preferred_element_type=jnp.float32)
        acc = term if acc is None else acc + term
    pre_ref[...] = acc
    step = 16

    def activate(i, carry):
        at = pl.ds(pl.multiple_of(i * step, step), step)
        u = pre_ref[at, :]
        tangent = jnp.tanh(SQRT_TWO_PI * (u + CUBIC * u * u * u))
        hidden_ref[at, :] = (0.5 * u * (1.0 + tangent)).astype(jnp.bfloat16)
        slope_ref[at, :] = (
            0.5 * (1.0 + tangent)
            + 0.5
            * u
            * (1.0 - tangent * tangent)
            * SQRT_TWO_PI
            * (1.0 + 3.0 * CUBIC * u * u)
        )
        return carry

    lax.fori_loop(0, slots // step, activate, 0)
    saves = [
        fetch(hidden_ref, hidden_out, sems.at[parts + 1]),
        fetch(slope_ref, slope_out, sems.at[parts + 2]),
    ]
    outer_copy.wait()
    for q in range(parts):
        outs_ref[q] = jnp.dot(
            hidden_ref[...], outer_ref[:, piece[q]], preferred_element_type=jnp.float32
        ).astype(jnp.bfloat16)
        saves.append(fetch(outs_ref.at[q], outs_out.at[q], sems.at[parts + 3 + q]))
    for copy in saves:
        copy.wait()


def backward_kernel(parts, me_ref, cot_ref, hidden_in, slope_in, inner_in, outer_in, *refs):
    in_refs = refs[:parts]
    hidden_ref, slope_ref, inner_ref, outer_ref, back_ref, grad_ref, pre_ref, sems = refs[parts:]
    slots, quarter = cot_ref.shape[1:]
    width = back_ref.shape[1]
    across = (((1,), (1,)), ((), ()))
    outer_copy = fetch(outer_in, outer_ref, sems.at[0])
    later = [
        fetch(source, target, sems.at[1 + i])
        for i, (source, target) in enumerate(
            ((slope_in, slope_ref), (hidden_in, hidden_ref), (inner_in, inner_ref))
        )
    ]
    outer_copy.wait()
    acc = None
    for q in range(parts):
        term = lax.dot_general(
            cot_ref[q],
            outer_ref[:, q * quarter : (q + 1) * quarter],
            across,
            preferred_element_type=jnp.float32,
        )
        acc = term if acc is None else acc + term
    back_ref[...] = acc
    for copy in later:
        copy.wait()
    step = 16

    def activate(i, carry):
        at = pl.ds(pl.multiple_of(i * step, step), step)
        back = back_ref[at, :]
        pre_ref[at, :] = (back * slope_ref[at, :]).astype(jnp.bfloat16)
        product = back * hidden_ref[at, :].astype(jnp.float32)
        folded = product[:, :128]
        for j in range(1, width // 128):
            folded = folded + product[:, j * 128 : (j + 1) * 128]
        grad_ref[at, :] = folded
        return carry

    lax.fori_loop(0, slots // step, activate, 0)
    gate = lax.dot_general(
        jnp.ones((8, 128), jnp.float32),
        grad_ref[...],
        across,
        precision=lax.Precision.HIGHEST,
        preferred_element_type=jnp.float32,
    )[:1, :]
    high = gate.astype(jnp.bfloat16).astype(jnp.float32)
    low = gate - high
    place = iota((EXTRA, quarter), 0)
    extra = jnp.zeros((EXTRA, quarter), jnp.float32)
    for j in range(slots // quarter):
        piece = slice(j * quarter, (j + 1) * quarter)
        extra = jnp.where(place == 2 * j, high[:, piece], extra)
        extra = jnp.where(place == 2 * j + 1, low[:, piece], extra)
    for shift in range(parts):
        of = quarter_of(lax.rem(me_ref[0] + shift, parts), quarter)
        in_refs[shift][:slots, :] = lax.dot_general(
            pre_ref[...], inner_ref[of, :], across, preferred_element_type=jnp.float32
        ).astype(jnp.bfloat16)
        in_refs[shift][slots:, :] = extra.astype(jnp.bfloat16)


def in_pairs(terms):
    wide = [t.astype(jnp.float32) for t in terms]
    half = len(wide) // 2
    if half == 0:
        return wide[0]
    return in_pairs([wide[i] + wide[i + half] for i in range(half)])


def add_kernel(outs_ref, *refs):
    in_refs, sum_ref = refs[:-1], refs[-1]
    parts, slots, quarter = outs_ref.shape
    step = 16

    def add(i, carry):
        at = pl.ds(pl.multiple_of(i * step, step), step)
        total = in_pairs([outs_ref[q, at, :] for q in range(parts)])
        other = in_pairs([ref[at, :] for ref in in_refs])
        sum_ref[at, :quarter] = total.astype(jnp.bfloat16)
        sum_ref[at, quarter : 2 * quarter] = other.astype(jnp.bfloat16)
        return carry

    lax.fori_loop(0, slots // step, add, 0)
    chunks = slots // quarter
    split = [ref[slots:, :].astype(jnp.float32) for ref in in_refs]
    extra = [
        in_pairs([part[2 * j : 2 * j + 1, :] + part[2 * j + 1 : 2 * j + 2, :] for part in split])
        for j in range(chunks)
    ]
    lane = iota((128, 128), 1)
    for j in range(slots // 128):
        at, lanes = divmod(j * 128, quarter)
        gate = column_of(extra[at][:, lanes : lanes + 128])
        high = gate.astype(jnp.bfloat16).astype(jnp.float32)
        low = gate - high
        sum_ref[j * 128 : (j + 1) * 128, 2 * quarter :] = jnp.where(
            lane == 0, high, jnp.where(lane == 1, low, 0.0)
        ).astype(jnp.bfloat16)


def table_kernel(experts, capacity, ids_ref, table_ref):
    rows = ids_ref.shape[1]
    positions = slot_positions(ids_ref[...], experts, capacity)
    slot = iota((rows, experts * capacity), 1)
    for k in range(TOP):
        hit = slot == column_of(positions[k])
        table_ref[k * rows : (k + 1) * rows, :] = jnp.where(hit, 1.0, 0.0).astype(jnp.bfloat16)


def combine_kernel(table_ref, gates_ref, back_ref, out_ref, in_ref, gate_ref):
    rows, quarter = out_ref.shape
    total = None
    for k in range(TOP):
        picked = jnp.dot(
            table_ref[k * rows : (k + 1) * rows, :],
            back_ref[...],
            preferred_element_type=jnp.float32,
        )
        term = column_of(gates_ref[k : k + 1, :]) * picked[:, : 2 * quarter]
        total = term if total is None else total + term
        gate = picked[:, 2 * quarter : 2 * quarter + 1] + picked[:, 2 * quarter + 1 : 2 * quarter + 2]
        gate_ref[k : k + 1, :] = row_of(gate)
    out_ref[...] = total[:, :quarter].astype(jnp.bfloat16)
    in_ref[...] = total[:, quarter:].astype(jnp.bfloat16)


def to_everyone(x, axis):
    peers = lax.axis_size(axis)
    return lax.all_to_all(jnp.broadcast_to(x[None], (peers, *x.shape)), axis, 0, 0, tiled=True)


def shift_by(x, axis, shift):
    peers = lax.axis_size(axis)
    return lax.ppermute(x, axis, [(i, (i + shift) % peers) for i in range(peers)])


def shifted(x, axis):
    return [shift_by(x, axis, shift) for shift in range(1, lax.axis_size(axis))]


def shape_of(shape, dtype):
    return jax.ShapeDtypeStruct(shape, dtype)


def in_hbm(x):
    return pltpu.with_memory_space_constraint(x, pltpu.HBM)


def exchange(tokens, cotangent, expert_ids, gate_values, inner_weight, outer_weight):
    rows, quarter = tokens.shape
    peers = lax.axis_size("expert")
    experts = peers * inner_weight.shape[0]
    capacity = 2 * rows * TOP // experts
    slots = experts * capacity
    parts = lax.axis_size("rep")
    inner, outer = in_hbm(inner_weight[0]), in_hbm(outer_weight[0])
    depth, width = inner.shape
    ids, gates = expert_ids.T, gate_values.T
    any_spec = pl.BlockSpec(memory_space=pltpu.HBM)
    vmem_spec = pl.BlockSpec(memory_space=pltpu.VMEM)
    half, full = jnp.bfloat16, jnp.float32

    packed = pl.pallas_call(
        lambda *refs: pack_kernel(experts, capacity, *refs),
        out_shape=shape_of((slots, 2 * quarter), half),
        in_specs=[any_spec] * 3,
        scratch_shapes=[
            pltpu.VMEM(ids.shape, ids.dtype),
            pltpu.VMEM(tokens.shape, tokens.dtype),
            pltpu.VMEM(cotangent.shape, cotangent.dtype),
            pltpu.SemaphoreType.DMA((3,)),
        ],
        compiler_params=PARAMS,
        name="pack",
    )(in_hbm(ids), in_hbm(tokens), in_hbm(cotangent))
    arrived = lax.all_to_all(
        packed.reshape(peers, -1, 2 * quarter), "expert", 0, 0, tiled=True
    ).reshape(slots, 2 * quarter)
    mine = arrived[:, :quarter]
    near = shifted(mine, "rep")
    all_cots = to_everyone(arrived[:, quarter:], "rep")
    table = pl.pallas_call(
        lambda *refs: table_kernel(experts, capacity, *refs),
        out_shape=shape_of((TOP * rows, slots), half),
        compiler_params=PARAMS,
        name="table",
    )(ids)
    me = lax.axis_index("rep").astype(jnp.int32).reshape(1)
    smem_spec = pl.BlockSpec(memory_space=pltpu.SMEM)

    outs, hidden, slope = pl.pallas_call(
        lambda *refs: forward_kernel(parts, *refs),
        out_shape=(
            pltpu.HBM((parts, slots, quarter), half),
            pltpu.HBM((slots, width), half),
            pltpu.HBM((slots, width), full),
        ),
        in_specs=[smem_spec, any_spec] + [vmem_spec] * (parts - 1) + [any_spec] * 2,
        out_specs=(any_spec, any_spec, any_spec),
        scratch_shapes=[
            pltpu.VMEM((slots, quarter), half),
            pltpu.VMEM((depth, width), half),
            pltpu.VMEM((width, depth), half),
            pltpu.VMEM((parts, slots, quarter), half),
            pltpu.VMEM((slots, width), half),
            pltpu.VMEM((slots, width), full),
            pltpu.VMEM((slots, width), full),
            pltpu.SemaphoreType.DMA((2 * parts + 4,)),
        ],
        compiler_params=PARAMS,
        name="forward",
    )(me, in_hbm(mine), *near, inner, outer)
    outs = lax.all_to_all(outs, "rep", 0, 0, tiled=True)
    own, *others = pl.pallas_call(
        lambda *refs: backward_kernel(parts, *refs),
        out_shape=(shape_of((slots + EXTRA, quarter), half),) * parts,
        in_specs=[smem_spec, vmem_spec] + [any_spec] * 4,
        scratch_shapes=[
            pltpu.VMEM((slots, width), half),
            pltpu.VMEM((slots, width), full),
            pltpu.VMEM((depth, width), half),
            pltpu.VMEM((width, depth), half),
            pltpu.VMEM((slots, width), full),
            pltpu.VMEM((slots, 128), full),
            pltpu.VMEM((slots, width), half),
            pltpu.SemaphoreType.DMA((4,)),
        ],
        compiler_params=PARAMS,
        name="backward",
    )(me, all_cots, in_hbm(hidden), in_hbm(slope), inner, outer)
    arrivals = [own] + [shift_by(x, "rep", 1 + i) for i, x in enumerate(others)]
    summed = pl.pallas_call(
        add_kernel,
        out_shape=shape_of((slots, 2 * quarter + 128), half),
        compiler_params=PARAMS,
        name="add",
    )(outs, *arrivals)
    back = lax.all_to_all(
        summed.reshape(peers, -1, 2 * quarter + 128), "expert", 0, 0, tiled=True
    ).reshape(slots, 2 * quarter + 128)
    output, input_grads, gate_grads = pl.pallas_call(
        combine_kernel,
        out_shape=(
            shape_of((rows, quarter), half),
            shape_of((rows, quarter), half),
            shape_of((TOP, rows), full),
        ),
        compiler_params=PARAMS,
        name="combine",
    )(table, gates, back)
    return output, input_grads, gate_grads.T


def solution(mesh):
    placed = (
        P("expert", "rep"),
        P("expert", "rep"),
        P("expert", None),
        P("expert", None),
        P("expert", None, "rep"),
        P("expert", "rep", None),
    )
    return jax.shard_map(
        exchange,
        mesh=mesh,
        in_specs=placed,
        out_specs=(P("expert", "rep"), P("expert", "rep"), P("expert", None)),
        check_vma=False,
    )
```

```python
import jax
import jax.numpy as jnp
from jax import lax
from jax.experimental import pallas as pl
from jax.experimental.pallas import tpu as pltpu
from jax.sharding import PartitionSpec as P

TOP = 2
EXTRA = 16

SQRT_TWO_PI = 0.7978845608028654
CUBIC = 0.044715

PARAMS = pltpu.CompilerParams(vmem_limit_bytes=24 * 1024 * 1024)


def iota(shape, dim):
    return lax.broadcasted_iota(jnp.int32, shape, dim)


def slot_positions(ids, experts, capacity):
    rows = ids.shape[1]
    of_expert = iota((experts, rows), 0)
    named = [of_expert == ids[k : k + 1, :] for k in range(TOP)]
    both = sum(jnp.where(m, 1.0, 0.0) for m in named)
    earlier = jnp.where(iota((rows, rows), 0) < iota((rows, rows), 1), 1.0, 0.0)
    before = jnp.dot(
        both.astype(jnp.bfloat16), earlier.astype(jnp.bfloat16), preferred_element_type=jnp.float32
    )
    ranks = [jnp.sum(jnp.where(m, before, 0.0), axis=0, keepdims=True) for m in named]
    return [ids[k : k + 1, :] * capacity + ranks[k].astype(jnp.int32) for k in range(TOP)]


def column_of(row):
    n = row.shape[1]
    eye = iota((n, n), 0) == iota((n, n), 1)
    return jnp.sum(jnp.where(eye, row, jnp.zeros_like(row)), axis=1, keepdims=True)


def row_of(column):
    n = column.shape[0]
    eye = iota((n, n), 0) == iota((n, n), 1)
    return jnp.sum(jnp.where(eye, column, jnp.zeros_like(column)), axis=0, keepdims=True)


def pack_kernel(
    experts, capacity, ids_in, token_in, cot_in, out_ref, ids_ref, token_ref, cot_ref, sems
):
    copies = [
        pltpu.make_async_copy(src, dst, sems.at[i])
        for i, (src, dst) in enumerate(
            ((ids_in, ids_ref), (token_in, token_ref), (cot_in, cot_ref))
        )
    ]
    for copy in copies:
        copy.start()
    copies[0].wait()
    quarter = token_ref.shape[1]
    positions = slot_positions(ids_ref[...], experts, capacity)
    slot = iota((experts * capacity, token_ref.shape[0]), 0)
    hit = slot == positions[0]
    for k in range(1, TOP):
        hit = hit | (slot == positions[k])
    table = jnp.where(hit, 1.0, 0.0).astype(jnp.bfloat16)
    for part, ref in enumerate((token_ref, cot_ref)):
        copies[1 + part].wait()
        out_ref[:, part * quarter : (part + 1) * quarter] = jnp.dot(
            table, ref[...], preferred_element_type=jnp.float32
        ).astype(jnp.bfloat16)


def spread_kernel(arrived_ref, rows_out, cots_out, sems):
    parts, _, quarter = rows_out.shape
    copies = [
        fetch(arrived_ref.at[:, :quarter], rows_out.at[q], sems.at[q]) for q in range(parts)
    ]
    copies.append(fetch(arrived_ref.at[:, quarter:], cots_out, sems.at[parts]))
    for copy in copies:
        copy.wait()


def fetch(source, target, sem):
    copy = pltpu.make_async_copy(source, target, sem)
    copy.start()
    return copy


def quarter_of(index, size):
    return pl.ds(pl.multiple_of(index * size, size), size)


def forward_kernel(
    rows_ref,
    inner_in,
    outer_in,
    outs_out,
    hidden_out,
    slope_out,
    inner_ref,
    outer_ref,
    outs_ref,
    hidden_ref,
    slope_ref,
    pre_ref,
    sems,
):
    parts, slots, quarter = rows_ref.shape
    piece = [slice(q * quarter, (q + 1) * quarter) for q in range(parts)]
    inner_copies = [
        fetch(inner_in.at[piece[q], :], inner_ref.at[piece[q], :], sems.at[q]) for q in range(parts)
    ]
    outer_copy = fetch(outer_in, outer_ref, sems.at[parts])
    acc = None
    for q in range(parts):
        inner_copies[q].wait()
        term = jnp.dot(rows_ref[q], inner_ref[piece[q], :], preferred_element_type=jnp.float32)
        acc = term if acc is None else acc + term
    pre_ref[...] = acc
    step = 16

    def activate(i, carry):
        at = pl.ds(pl.multiple_of(i * step, step), step)
        u = pre_ref[at, :]
        square = u * u
        tangent = jnp.tanh(u * (SQRT_TWO_PI + (SQRT_TWO_PI * CUBIC) * square))
        share = 0.5 + 0.5 * tangent
        result = u * share
        hidden_ref[at, :] = result.astype(jnp.bfloat16)
        slope_ref[at, :] = (
            share
            + result
            * (1.0 - share)
            * (2.0 * SQRT_TWO_PI + (6.0 * SQRT_TWO_PI * CUBIC) * square)
        ).astype(jnp.bfloat16)
        return carry

    lax.fori_loop(0, slots // step, activate, 0)
    saves = [
        fetch(hidden_ref, hidden_out, sems.at[parts + 1]),
        fetch(slope_ref, slope_out, sems.at[parts + 2]),
    ]
    outer_copy.wait()
    for q in range(parts):
        outs_ref[q] = jnp.dot(
            hidden_ref[...], outer_ref[:, piece[q]], preferred_element_type=jnp.float32
        ).astype(jnp.bfloat16)
        saves.append(fetch(outs_ref.at[q], outs_out.at[q], sems.at[parts + 3 + q]))
    for copy in saves:
        copy.wait()


def backward_kernel(parts, me_ref, *refs):
    cot_ins, (hidden_in, slope_in, inner_in, outer_in) = refs[:parts], refs[parts : parts + 4]
    in_outs = refs[parts + 4 : 2 * parts + 4]
    (
        cot_ref,
        hidden_ref,
        slope_ref,
        inner_ref,
        outer_ref,
        in_ref,
        back_ref,
        grad_ref,
        pre_ref,
        sems,
    ) = refs[2 * parts + 4 :]
    slots, quarter = cot_ref.shape[1:]
    width = back_ref.shape[1]
    across = (((1,), (1,)), ((), ()))
    piece = [slice(q * quarter, (q + 1) * quarter) for q in range(parts)]
    first = [
        (
            fetch(cot_ins[shift], cot_ref.at[shift], sems.at[2 * shift]),
            fetch(
                outer_in.at[:, quarter_of(lax.rem(me_ref[0] + parts - shift, parts), quarter)],
                outer_ref.at[:, piece[shift]],
                sems.at[2 * shift + 1],
            ),
        )
        for shift in range(parts)
    ]
    copies = [
        fetch(source, target, sems.at[2 * parts + i])
        for i, (source, target) in enumerate(
            ((slope_in, slope_ref), (hidden_in, hidden_ref), (inner_in, inner_ref))
        )
    ]
    acc = None
    for shift in range(parts):
        for copy in first[shift]:
            copy.wait()
        term = lax.dot_general(
            cot_ref[shift],
            outer_ref[:, piece[shift]],
            across,
            preferred_element_type=jnp.float32,
        )
        acc = term if acc is None else acc + term
    back_ref[...] = acc
    copies[0].wait()
    copies[1].wait()
    step = 16

    def activate(i, carry):
        at = pl.ds(pl.multiple_of(i * step, step), step)
        back = back_ref[at, :]
        pre_ref[at, :] = (back * slope_ref[at, :].astype(jnp.float32)).astype(jnp.bfloat16)
        product = back * hidden_ref[at, :].astype(jnp.float32)
        folded = product[:, :128]
        for j in range(1, width // 128):
            folded = folded + product[:, j * 128 : (j + 1) * 128]
        grad_ref[at, :] = folded
        return carry

    lax.fori_loop(0, slots // step, activate, 0)
    gate = lax.dot_general(
        jnp.ones((8, 128), jnp.float32),
        grad_ref[...],
        across,
        precision=lax.Precision.HIGHEST,
        preferred_element_type=jnp.float32,
    )[:1, :]
    high = gate.astype(jnp.bfloat16).astype(jnp.float32)
    low = gate - high
    place = iota((EXTRA, quarter), 0)
    extra = jnp.zeros((EXTRA, quarter), jnp.float32)
    for j in range(slots // quarter):
        extra = jnp.where(place == 2 * j, high[:, piece[j]], extra)
        extra = jnp.where(place == 2 * j + 1, low[:, piece[j]], extra)
    copies[2].wait()
    saves = []
    for shift in range(parts):
        of = quarter_of(lax.rem(me_ref[0] + shift, parts), quarter)
        in_ref[shift, :slots, :] = lax.dot_general(
            pre_ref[...], inner_ref[of, :], across, preferred_element_type=jnp.float32
        ).astype(jnp.bfloat16)
        in_ref[shift, slots:, :] = extra.astype(jnp.bfloat16)
        saves.append(fetch(in_ref.at[shift], in_outs[shift], sems.at[2 * parts + 3 + shift]))
    for copy in saves:
        copy.wait()


def in_pairs(terms):
    wide = [t.astype(jnp.float32) for t in terms]
    half = len(wide) // 2
    if half == 0:
        return wide[0]
    return in_pairs([wide[i] + wide[i + half] for i in range(half)])


def add_outs_kernel(outs_ref, own_in, sum_ref, own_ref, sem):
    copy = fetch(own_in, own_ref, sem)
    sum_ref[...] = in_pairs([outs_ref[q] for q in range(outs_ref.shape[0])]).astype(jnp.bfloat16)
    copy.wait()


def add_kernel(out_ref, *refs):
    in_refs, sum_ref = refs[:-1], refs[-1]
    slots, quarter = out_ref.shape
    step = 16

    def add(i, carry):
        at = pl.ds(pl.multiple_of(i * step, step), step)
        sum_ref[at, :quarter] = out_ref[at, :]
        sum_ref[at, quarter : 2 * quarter] = in_pairs([ref[at, :] for ref in in_refs]).astype(
            jnp.bfloat16
        )
        return carry

    lax.fori_loop(0, slots // step, add, 0)
    chunks = slots // quarter
    split = [ref[slots:, :].astype(jnp.float32) for ref in in_refs]
    extra = [
        in_pairs([part[2 * j : 2 * j + 1, :] + part[2 * j + 1 : 2 * j + 2, :] for part in split])
        for j in range(chunks)
    ]
    lane = iota((128, 128), 1)
    for j in range(slots // 128):
        at, lanes = divmod(j * 128, quarter)
        gate = column_of(extra[at][:, lanes : lanes + 128])
        high = gate.astype(jnp.bfloat16).astype(jnp.float32)
        low = gate - high
        sum_ref[j * 128 : (j + 1) * 128, 2 * quarter :] = jnp.where(
            lane == 0, high, jnp.where(lane == 1, low, 0.0)
        ).astype(jnp.bfloat16)


def table_kernel(experts, capacity, k, ids_ref, table_ref):
    rows = ids_ref.shape[1]
    position = slot_positions(ids_ref[...], experts, capacity)[k]
    hit = iota((rows, experts * capacity), 1) == column_of(position)
    table_ref[...] = jnp.where(hit, 1.0, 0.0).astype(jnp.bfloat16)


def combine_kernel(*refs):
    table_refs, gates_ref, back_ref = refs[:TOP], refs[TOP], refs[TOP + 1]
    out_ref, in_ref, gate_ref = refs[TOP + 2 :]
    quarter = out_ref.shape[1]
    total = None
    for k in range(TOP):
        picked = jnp.dot(table_refs[k][...], back_ref[...], preferred_element_type=jnp.float32)
        term = column_of(gates_ref[k : k + 1, :]) * picked[:, : 2 * quarter]
        total = term if total is None else total + term
        gate = picked[:, 2 * quarter : 2 * quarter + 1] + picked[:, 2 * quarter + 1 : 2 * quarter + 2]
        gate_ref[k : k + 1, :] = row_of(gate)
    out_ref[...] = total[:, :quarter].astype(jnp.bfloat16)
    in_ref[...] = total[:, quarter:].astype(jnp.bfloat16)


def shift_by(x, axis, shift):
    peers = lax.axis_size(axis)
    return lax.ppermute(x, axis, [(i, (i + shift) % peers) for i in range(peers)])


def sent_on(pieces, axis):
    order = sorted(range(1, len(pieces)), key=lambda s: -min(s, len(pieces) - s))
    moved = {0: pieces[0]} | {s: shift_by(pieces[s], axis, s) for s in order}
    return [moved[s] for s in range(len(pieces))]


def shape_of(shape, dtype):
    return jax.ShapeDtypeStruct(shape, dtype)


def in_hbm(x):
    return pltpu.with_memory_space_constraint(x, pltpu.HBM)


def exchange(tokens, cotangent, expert_ids, gate_values, inner_weight, outer_weight):
    rows, quarter = tokens.shape
    peers = lax.axis_size("expert")
    experts = peers * inner_weight.shape[0]
    capacity = 2 * rows * TOP // experts
    slots = experts * capacity
    parts = lax.axis_size("rep")
    inner, outer = inner_weight[0], outer_weight[0]
    depth, width = inner.shape
    ids, gates = expert_ids.T, gate_values.T
    any_spec = pl.BlockSpec(memory_space=pltpu.HBM)
    vmem_spec = pl.BlockSpec(memory_space=pltpu.VMEM)
    half, full = jnp.bfloat16, jnp.float32

    packed = pl.pallas_call(
        lambda *refs: pack_kernel(experts, capacity, *refs),
        out_shape=shape_of((slots, 2 * quarter), half),
        in_specs=[any_spec] * 3,
        scratch_shapes=[
            pltpu.VMEM(ids.shape, ids.dtype),
            pltpu.VMEM(tokens.shape, tokens.dtype),
            pltpu.VMEM(cotangent.shape, cotangent.dtype),
            pltpu.SemaphoreType.DMA((3,)),
        ],
        compiler_params=PARAMS,
        name="pack",
    )(in_hbm(ids), in_hbm(tokens), in_hbm(cotangent))
    arrived = lax.all_to_all(
        packed.reshape(peers, -1, 2 * quarter), "expert", 0, 0, tiled=True
    ).reshape(slots, 2 * quarter)
    copied, cots = pl.pallas_call(
        spread_kernel,
        out_shape=(pltpu.HBM((parts, slots, quarter), half), pltpu.HBM((slots, quarter), half)),
        in_specs=[vmem_spec],
        out_specs=(any_spec, any_spec),
        scratch_shapes=[pltpu.SemaphoreType.DMA((parts + 1,))],
        compiler_params=PARAMS,
        name="spread",
    )(arrived)
    all_rows = lax.all_to_all(copied, "rep", 0, 0, tiled=True)
    all_cots = sent_on([cots] * parts, "rep")
    tables = []
    for k in range(TOP):
        tables.append(
            pl.pallas_call(
                lambda *refs: table_kernel(experts, capacity, k, *refs),
                out_shape=shape_of((rows, slots), half),
                compiler_params=PARAMS,
            )(ids)
        )
    me = lax.axis_index("rep").astype(jnp.int32).reshape(1)
    smem_spec = pl.BlockSpec(memory_space=pltpu.SMEM)

    outs, hidden, slope = pl.pallas_call(
        forward_kernel,
        out_shape=(
            pltpu.HBM((parts, slots, quarter), half),
            pltpu.HBM((slots, width), half),
            pltpu.HBM((slots, width), half),
        ),
        in_specs=[vmem_spec, any_spec, any_spec],
        out_specs=(any_spec,) * 3,
        scratch_shapes=[
            pltpu.VMEM((depth, width), half),
            pltpu.VMEM((width, depth), half),
            pltpu.VMEM((parts, slots, quarter), half),
            pltpu.VMEM((slots, width), half),
            pltpu.VMEM((slots, width), half),
            pltpu.VMEM((slots, width), full),
            pltpu.SemaphoreType.DMA((2 * parts + 3,)),
        ],
        compiler_params=PARAMS,
        name="forward",
    )(all_rows, in_hbm(inner), in_hbm(outer))
    outs = lax.all_to_all(outs, "rep", 0, 0, tiled=True)
    ins = pl.pallas_call(
        lambda *refs: backward_kernel(parts, *refs),
        out_shape=(pltpu.HBM((slots + EXTRA, quarter), half),) * parts,
        in_specs=[smem_spec] + [any_spec] * (parts + 4),
        out_specs=(any_spec,) * parts,
        scratch_shapes=[
            pltpu.VMEM((parts, slots, quarter), half),
            pltpu.VMEM((slots, width), half),
            pltpu.VMEM((slots, width), half),
            pltpu.VMEM((depth, width), half),
            pltpu.VMEM((width, depth), half),
            pltpu.VMEM((parts, slots + EXTRA, quarter), half),
            pltpu.VMEM((slots, width), full),
            pltpu.VMEM((slots, 128), full),
            pltpu.VMEM((slots, width), half),
            pltpu.SemaphoreType.DMA((3 * parts + 3,)),
        ],
        compiler_params=PARAMS,
        name="backward",
    )(me, *all_cots, *[in_hbm(x) for x in (hidden, slope, inner, outer)])
    arrivals = sent_on(ins, "rep")
    out, own = pl.pallas_call(
        add_outs_kernel,
        out_shape=(shape_of((slots, quarter), half), shape_of((slots + EXTRA, quarter), half)),
        in_specs=[vmem_spec, any_spec],
        scratch_shapes=[pltpu.SemaphoreType.DMA(())],
        compiler_params=PARAMS,
        name="add_outs",
    )(outs, in_hbm(arrivals[0]))
    summed = pl.pallas_call(
        add_kernel,
        out_shape=shape_of((slots, 2 * quarter + 128), half),
        compiler_params=PARAMS,
        name="add",
    )(out, own, *arrivals[1:])
    back = lax.all_to_all(
        summed.reshape(peers, -1, 2 * quarter + 128), "expert", 0, 0, tiled=True
    ).reshape(slots, 2 * quarter + 128)
    output, input_grads, gate_grads = pl.pallas_call(
        combine_kernel,
        out_shape=(
            shape_of((rows, quarter), half),
            shape_of((rows, quarter), half),
            shape_of((TOP, rows), full),
        ),
        compiler_params=PARAMS,
        name="combine",
    )(*tables, gates, back)
    return output, input_grads, gate_grads.T


def solution(mesh):
    placed = (
        P("expert", "rep"),
        P("expert", "rep"),
        P("expert", None),
        P("expert", None),
        P("expert", None, "rep"),
        P("expert", "rep", None),
    )
    return jax.shard_map(
        exchange,
        mesh=mesh,
        in_specs=placed,
        out_specs=(P("expert", "rep"), P("expert", "rep"), P("expert", None)),
        check_vma=False,
    )
```

```python
import jax
import jax.numpy as jnp
from jax import lax
from jax.experimental import pallas as pl
from jax.experimental.pallas import tpu as pltpu
from jax.sharding import PartitionSpec as P

TOP = 2
EXTRA = 16

SQRT_TWO_PI = 0.7978845608028654
CUBIC = 0.044715

PARAMS = pltpu.CompilerParams(vmem_limit_bytes=24 * 1024 * 1024)


def iota(shape, dim):
    return lax.broadcasted_iota(jnp.int32, shape, dim)


def slot_positions(ids, experts, capacity):
    rows = ids.shape[1]
    of_expert = iota((experts, rows), 0)
    named = [of_expert == ids[k : k + 1, :] for k in range(TOP)]
    both = sum(jnp.where(m, 1.0, 0.0) for m in named)
    earlier = jnp.where(iota((rows, rows), 0) < iota((rows, rows), 1), 1.0, 0.0)
    before = jnp.dot(
        both.astype(jnp.bfloat16), earlier.astype(jnp.bfloat16), preferred_element_type=jnp.float32
    )
    ranks = [jnp.sum(jnp.where(m, before, 0.0), axis=0, keepdims=True) for m in named]
    return [ids[k : k + 1, :] * capacity + ranks[k].astype(jnp.int32) for k in range(TOP)]


def column_of(row):
    n = row.shape[1]
    eye = iota((n, n), 0) == iota((n, n), 1)
    return jnp.sum(jnp.where(eye, row, jnp.zeros_like(row)), axis=1, keepdims=True)


def row_of(column):
    n = column.shape[0]
    eye = iota((n, n), 0) == iota((n, n), 1)
    return jnp.sum(jnp.where(eye, column, jnp.zeros_like(column)), axis=0, keepdims=True)


def pack_kernel(
    experts, capacity, ids_in, token_in, cot_in, out_ref, ids_ref, token_ref, cot_ref, sems
):
    copies = [
        pltpu.make_async_copy(src, dst, sems.at[i])
        for i, (src, dst) in enumerate(
            ((ids_in, ids_ref), (token_in, token_ref), (cot_in, cot_ref))
        )
    ]
    for copy in copies:
        copy.start()
    copies[0].wait()
    quarter = token_ref.shape[1]
    positions = slot_positions(ids_ref[...], experts, capacity)
    slot = iota((experts * capacity, token_ref.shape[0]), 0)
    hit = slot == positions[0]
    for k in range(1, TOP):
        hit = hit | (slot == positions[k])
    table = jnp.where(hit, 1.0, 0.0).astype(jnp.bfloat16)
    for part, ref in enumerate((token_ref, cot_ref)):
        copies[1 + part].wait()
        out_ref[:, part * quarter : (part + 1) * quarter] = jnp.dot(
            table, ref[...], preferred_element_type=jnp.float32
        ).astype(jnp.bfloat16)


def spread_kernel(arrived_ref, rows_out, cots_out, sems):
    parts, _, quarter = rows_out.shape
    copies = [
        fetch(arrived_ref.at[:, :quarter], rows_out.at[q], sems.at[q]) for q in range(parts)
    ]
    copies.append(fetch(arrived_ref.at[:, quarter:], cots_out, sems.at[parts]))
    for copy in copies:
        copy.wait()


def fetch(source, target, sem):
    copy = pltpu.make_async_copy(source, target, sem)
    copy.start()
    return copy


def quarter_of(index, size):
    return pl.ds(pl.multiple_of(index * size, size), size)


def forward_kernel(
    rows_ref,
    inner_ref,
    outer_in,
    outs_out,
    hidden_out,
    slope_out,
    outer_ref,
    outs_ref,
    hidden_ref,
    slope_ref,
    pre_ref,
    sems,
):
    parts, slots, quarter = rows_ref.shape
    piece = [slice(q * quarter, (q + 1) * quarter) for q in range(parts)]
    outer_copy = fetch(outer_in, outer_ref, sems.at[parts])
    acc = None
    for q in range(parts):
        term = jnp.dot(rows_ref[q], inner_ref[piece[q], :], preferred_element_type=jnp.float32)
        acc = term if acc is None else acc + term
    pre_ref[...] = acc
    step = 32

    def activate(i, carry):
        at = pl.ds(pl.multiple_of(i * step, step), step)
        u = pre_ref[at, :]
        square = u * u
        tangent = jnp.tanh(u * (SQRT_TWO_PI + (SQRT_TWO_PI * CUBIC) * square))
        share = 0.5 + 0.5 * tangent
        result = u * share
        hidden_ref[at, :] = result.astype(jnp.bfloat16)
        slope_ref[at, :] = (
            share
            + result
            * (1.0 - share)
            * (2.0 * SQRT_TWO_PI + (6.0 * SQRT_TWO_PI * CUBIC) * square)
        ).astype(jnp.bfloat16)
        return carry

    lax.fori_loop(0, slots // step, activate, 0)
    saves = [
        fetch(hidden_ref, hidden_out, sems.at[parts + 1]),
        fetch(slope_ref, slope_out, sems.at[parts + 2]),
    ]
    outer_copy.wait()
    for q in range(parts):
        outs_ref[q] = jnp.dot(
            hidden_ref[...], outer_ref[:, piece[q]], preferred_element_type=jnp.float32
        ).astype(jnp.bfloat16)
        saves.append(fetch(outs_ref.at[q], outs_out.at[q], sems.at[parts + 3 + q]))
    for copy in saves:
        copy.wait()


def backward_kernel(parts, me_ref, *refs):
    cot_ins, (hidden_in, slope_in, inner_in, outer_ref) = refs[:parts], refs[parts : parts + 4]
    in_outs = refs[parts + 4 : 2 * parts + 4]
    (
        cot_ref,
        hidden_ref,
        slope_ref,
        inner_ref,
        in_ref,
        back_ref,
        grad_ref,
        pre_ref,
        sems,
    ) = refs[2 * parts + 4 :]
    slots, quarter = cot_ref.shape[1:]
    width = back_ref.shape[1]
    across = (((1,), (1,)), ((), ()))
    piece = [slice(q * quarter, (q + 1) * quarter) for q in range(parts)]
    first = [fetch(cot_ins[i], cot_ref.at[i], sems.at[i]) for i in range(parts)]
    copies = [
        fetch(source, target, sems.at[2 * parts + i])
        for i, (source, target) in enumerate(
            ((slope_in, slope_ref), (hidden_in, hidden_ref), (inner_in, inner_ref))
        )
    ]
    acc = None
    for shift in range(parts):
        first[shift].wait()
        of = quarter_of(lax.rem(me_ref[0] + parts - shift, parts), quarter)
        term = lax.dot_general(
            cot_ref[shift],
            outer_ref[:, of],
            across,
            preferred_element_type=jnp.float32,
        )
        acc = term if acc is None else acc + term
    back_ref[...] = acc
    copies[0].wait()
    copies[1].wait()
    step = 16

    def activate(i, carry):
        at = pl.ds(pl.multiple_of(i * step, step), step)
        back = back_ref[at, :]
        pre_ref[at, :] = (back * slope_ref[at, :].astype(jnp.float32)).astype(jnp.bfloat16)
        product = back * hidden_ref[at, :].astype(jnp.float32)
        folded = product[:, :128]
        for j in range(1, width // 128):
            folded = folded + product[:, j * 128 : (j + 1) * 128]
        grad_ref[at, :] = folded
        return carry

    lax.fori_loop(0, slots // step, activate, 0)
    gate = lax.dot_general(
        jnp.ones((8, 128), jnp.float32),
        grad_ref[...],
        across,
        precision=lax.Precision.HIGHEST,
        preferred_element_type=jnp.float32,
    )[:1, :]
    high = gate.astype(jnp.bfloat16).astype(jnp.float32)
    low = gate - high
    place = iota((EXTRA, quarter), 0)
    extra = jnp.zeros((EXTRA, quarter), jnp.float32)
    for j in range(slots // quarter):
        extra = jnp.where(place == 2 * j, high[:, piece[j]], extra)
        extra = jnp.where(place == 2 * j + 1, low[:, piece[j]], extra)
    copies[2].wait()
    saves = []
    for shift in range(parts):
        of = quarter_of(lax.rem(me_ref[0] + shift, parts), quarter)
        in_ref[shift, :slots, :] = lax.dot_general(
            pre_ref[...], inner_ref[of, :], across, preferred_element_type=jnp.float32
        ).astype(jnp.bfloat16)
        in_ref[shift, slots:, :] = extra.astype(jnp.bfloat16)
        saves.append(fetch(in_ref.at[shift], in_outs[shift], sems.at[2 * parts + 3 + shift]))
    for copy in saves:
        copy.wait()


def in_pairs(terms):
    wide = [t.astype(jnp.float32) for t in terms]
    half = len(wide) // 2
    if half == 0:
        return wide[0]
    return in_pairs([wide[i] + wide[i + half] for i in range(half)])


def add_outs_kernel(outs_ref, own_in, sum_ref, own_ref, sem):
    copy = fetch(own_in, own_ref, sem)
    sum_ref[...] = in_pairs([outs_ref[q] for q in range(outs_ref.shape[0])]).astype(jnp.bfloat16)
    copy.wait()


def add_kernel(out_ref, *refs):
    in_refs, sum_ref = refs[:-1], refs[-1]
    slots, quarter = out_ref.shape
    step = 16

    def add(i, carry):
        at = pl.ds(pl.multiple_of(i * step, step), step)
        sum_ref[at, :quarter] = out_ref[at, :]
        sum_ref[at, quarter : 2 * quarter] = in_pairs([ref[at, :] for ref in in_refs]).astype(
            jnp.bfloat16
        )
        return carry

    lax.fori_loop(0, slots // step, add, 0)
    chunks = slots // quarter
    split = [ref[slots:, :].astype(jnp.float32) for ref in in_refs]
    extra = [
        in_pairs([part[2 * j : 2 * j + 1, :] + part[2 * j + 1 : 2 * j + 2, :] for part in split])
        for j in range(chunks)
    ]
    lane = iota((128, 128), 1)
    for j in range(slots // 128):
        at, lanes = divmod(j * 128, quarter)
        gate = column_of(extra[at][:, lanes : lanes + 128])
        high = gate.astype(jnp.bfloat16).astype(jnp.float32)
        low = gate - high
        sum_ref[j * 128 : (j + 1) * 128, 2 * quarter :] = jnp.where(
            lane == 0, high, jnp.where(lane == 1, low, 0.0)
        ).astype(jnp.bfloat16)


def table_kernel(experts, capacity, k, ids_ref, table_ref):
    rows = ids_ref.shape[1]
    position = slot_positions(ids_ref[...], experts, capacity)[k]
    hit = iota((rows, experts * capacity), 1) == column_of(position)
    table_ref[...] = jnp.where(hit, 1.0, 0.0).astype(jnp.bfloat16)


def combine_kernel(*refs):
    table_refs, gates_ref, back_ref = refs[:TOP], refs[TOP], refs[TOP + 1]
    out_ref, in_ref, gate_ref = refs[TOP + 2 :]
    quarter = out_ref.shape[1]
    total = None
    for k in range(TOP):
        picked = jnp.dot(table_refs[k][...], back_ref[...], preferred_element_type=jnp.float32)
        term = column_of(gates_ref[k : k + 1, :]) * picked[:, : 2 * quarter]
        total = term if total is None else total + term
        gate = picked[:, 2 * quarter : 2 * quarter + 1] + picked[:, 2 * quarter + 1 : 2 * quarter + 2]
        gate_ref[k : k + 1, :] = row_of(gate)
    out_ref[...] = total[:, :quarter].astype(jnp.bfloat16)
    in_ref[...] = total[:, quarter:].astype(jnp.bfloat16)


def shift_by(x, axis, shift):
    peers = lax.axis_size(axis)
    return lax.ppermute(x, axis, [(i, (i + shift) % peers) for i in range(peers)])


def sent_on(pieces, axis):
    moved = [pieces[0]]
    for shift in range(1, len(pieces)):
        moved.append(shift_by(pieces[shift], axis, shift))
    return moved


def shape_of(shape, dtype):
    return jax.ShapeDtypeStruct(shape, dtype)


def in_hbm(x):
    return pltpu.with_memory_space_constraint(x, pltpu.HBM)


def exchange(tokens, cotangent, expert_ids, gate_values, inner_weight, outer_weight):
    rows, quarter = tokens.shape
    peers = lax.axis_size("expert")
    experts = peers * inner_weight.shape[0]
    capacity = 2 * rows * TOP // experts
    slots = experts * capacity
    parts = lax.axis_size("rep")
    inner, outer = inner_weight[0], outer_weight[0]
    depth, width = inner.shape
    ids, gates = expert_ids.T, gate_values.T
    any_spec = pl.BlockSpec(memory_space=pltpu.HBM)
    vmem_spec = pl.BlockSpec(memory_space=pltpu.VMEM)
    half, full = jnp.bfloat16, jnp.float32

    packed = pl.pallas_call(
        lambda *refs: pack_kernel(experts, capacity, *refs),
        out_shape=shape_of((slots, 2 * quarter), half),
        in_specs=[any_spec] * 3,
        scratch_shapes=[
            pltpu.VMEM(ids.shape, ids.dtype),
            pltpu.VMEM(tokens.shape, tokens.dtype),
            pltpu.VMEM(cotangent.shape, cotangent.dtype),
            pltpu.SemaphoreType.DMA((3,)),
        ],
        compiler_params=PARAMS,
        name="pack",
    )(in_hbm(ids), in_hbm(tokens), in_hbm(cotangent))
    arrived = lax.all_to_all(
        packed.reshape(peers, -1, 2 * quarter), "expert", 0, 0, tiled=True
    ).reshape(slots, 2 * quarter)
    copied, cots = pl.pallas_call(
        spread_kernel,
        out_shape=(pltpu.HBM((parts, slots, quarter), half), pltpu.HBM((slots, quarter), half)),
        in_specs=[vmem_spec],
        out_specs=(any_spec, any_spec),
        scratch_shapes=[pltpu.SemaphoreType.DMA((parts + 1,))],
        compiler_params=PARAMS,
        name="spread",
    )(arrived)
    all_rows = lax.all_to_all(copied, "rep", 0, 0, tiled=True)
    all_cots = sent_on([cots] * parts, "rep")
    tables = []
    for k in range(TOP):
        tables.append(
            pl.pallas_call(
                lambda *refs: table_kernel(experts, capacity, k, *refs),
                out_shape=shape_of((rows, slots), half),
                compiler_params=PARAMS,
            )(ids)
        )
    me = lax.axis_index("rep").astype(jnp.int32).reshape(1)
    smem_spec = pl.BlockSpec(memory_space=pltpu.SMEM)

    outs, hidden, slope = pl.pallas_call(
        forward_kernel,
        out_shape=(
            pltpu.HBM((parts, slots, quarter), half),
            pltpu.HBM((slots, width), half),
            pltpu.HBM((slots, width), half),
        ),
        in_specs=[vmem_spec, vmem_spec, any_spec],
        out_specs=(any_spec,) * 3,
        scratch_shapes=[
            pltpu.VMEM((width, depth), half),
            pltpu.VMEM((parts, slots, quarter), half),
            pltpu.VMEM((slots, width), half),
            pltpu.VMEM((slots, width), half),
            pltpu.VMEM((slots, width), full),
            pltpu.SemaphoreType.DMA((2 * parts + 3,)),
        ],
        compiler_params=PARAMS,
        name="forward",
    )(all_rows, inner, in_hbm(outer))
    outs = lax.all_to_all(outs, "rep", 0, 0, tiled=True)
    ins = pl.pallas_call(
        lambda *refs: backward_kernel(parts, *refs),
        out_shape=(pltpu.HBM((slots + EXTRA, quarter), half),) * parts,
        in_specs=[smem_spec] + [any_spec] * (parts + 3) + [vmem_spec],
        out_specs=(any_spec,) * parts,
        scratch_shapes=[
            pltpu.VMEM((parts, slots, quarter), half),
            pltpu.VMEM((slots, width), half),
            pltpu.VMEM((slots, width), half),
            pltpu.VMEM((depth, width), half),
            pltpu.VMEM((parts, slots + EXTRA, quarter), half),
            pltpu.VMEM((slots, width), full),
            pltpu.VMEM((slots, 128), full),
            pltpu.VMEM((slots, width), half),
            pltpu.SemaphoreType.DMA((3 * parts + 3,)),
        ],
        compiler_params=PARAMS,
        name="backward",
    )(me, *all_cots, *[in_hbm(x) for x in (hidden, slope, inner)], outer)
    arrivals = sent_on(ins, "rep")
    out, own = pl.pallas_call(
        add_outs_kernel,
        out_shape=(shape_of((slots, quarter), half), shape_of((slots + EXTRA, quarter), half)),
        in_specs=[vmem_spec, any_spec],
        scratch_shapes=[pltpu.SemaphoreType.DMA(())],
        compiler_params=PARAMS,
        name="add_outs",
    )(outs, in_hbm(arrivals[0]))
    summed = pl.pallas_call(
        add_kernel,
        out_shape=shape_of((slots, 2 * quarter + 128), half),
        compiler_params=PARAMS,
        name="add",
    )(out, own, *arrivals[1:])
    back = lax.all_to_all(
        summed.reshape(peers, -1, 2 * quarter + 128), "expert", 0, 0, tiled=True
    ).reshape(slots, 2 * quarter + 128)
    output, input_grads, gate_grads = pl.pallas_call(
        combine_kernel,
        out_shape=(
            shape_of((rows, quarter), half),
            shape_of((rows, quarter), half),
            shape_of((TOP, rows), full),
        ),
        compiler_params=PARAMS,
        name="combine",
    )(*tables, gates, back)
    return output, input_grads, gate_grads.T


def solution(mesh):
    placed = (
        P("expert", "rep"),
        P("expert", "rep"),
        P("expert", None),
        P("expert", None),
        P("expert", None, "rep"),
        P("expert", "rep", None),
    )
    return jax.shard_map(
        exchange,
        mesh=mesh,
        in_specs=placed,
        out_specs=(P("expert", "rep"), P("expert", "rep"), P("expert", None)),
        check_vma=False,
    )
```

```python
import jax
import jax.numpy as jnp
from jax import lax
from jax.experimental import pallas as pl
from jax.experimental.pallas import tpu as pltpu
from jax.sharding import PartitionSpec as P

TOP = 2
EXTRA = 16

SQRT_TWO_PI = 0.7978845608028654
CUBIC = 0.044715

PARAMS = pltpu.CompilerParams(vmem_limit_bytes=24 * 1024 * 1024)


def iota(shape, dim):
    return lax.broadcasted_iota(jnp.int32, shape, dim)


def slot_positions(ids, experts, capacity):
    rows = ids.shape[1]
    of_expert = iota((experts, rows), 0)
    named = [of_expert == ids[k : k + 1, :] for k in range(TOP)]
    both = sum(jnp.where(m, 1.0, 0.0) for m in named)
    earlier = jnp.where(iota((rows, rows), 0) < iota((rows, rows), 1), 1.0, 0.0)
    before = jnp.dot(
        both.astype(jnp.bfloat16), earlier.astype(jnp.bfloat16), preferred_element_type=jnp.float32
    )
    ranks = [jnp.sum(jnp.where(m, before, 0.0), axis=0, keepdims=True) for m in named]
    return [ids[k : k + 1, :] * capacity + ranks[k].astype(jnp.int32) for k in range(TOP)]


def column_of(row):
    n = row.shape[1]
    eye = iota((n, n), 0) == iota((n, n), 1)
    return jnp.sum(jnp.where(eye, row, jnp.zeros_like(row)), axis=1, keepdims=True)


def row_of(column):
    n = column.shape[0]
    eye = iota((n, n), 0) == iota((n, n), 1)
    return jnp.sum(jnp.where(eye, column, jnp.zeros_like(column)), axis=0, keepdims=True)


def pack_kernel(
    experts, capacity, ids_in, token_in, cot_in, out_ref, ids_ref, token_ref, cot_ref, sems
):
    copies = [
        pltpu.make_async_copy(src, dst, sems.at[i])
        for i, (src, dst) in enumerate(
            ((ids_in, ids_ref), (token_in, token_ref), (cot_in, cot_ref))
        )
    ]
    for copy in copies:
        copy.start()
    copies[0].wait()
    quarter = token_ref.shape[1]
    positions = slot_positions(ids_ref[...], experts, capacity)
    slot = iota((experts * capacity, token_ref.shape[0]), 0)
    hit = slot == positions[0]
    for k in range(1, TOP):
        hit = hit | (slot == positions[k])
    table = jnp.where(hit, 1.0, 0.0).astype(jnp.bfloat16)
    for part, ref in enumerate((token_ref, cot_ref)):
        copies[1 + part].wait()
        out_ref[:, part * quarter : (part + 1) * quarter] = jnp.dot(
            table, ref[...], preferred_element_type=jnp.float32
        ).astype(jnp.bfloat16)


def spread_kernel(arrived_ref, rows_out, cots_out, sems):
    parts, _, quarter = rows_out.shape
    copies = [
        fetch(arrived_ref.at[:, :quarter], rows_out.at[q], sems.at[q]) for q in range(parts)
    ]
    copies.append(fetch(arrived_ref.at[:, quarter:], cots_out, sems.at[parts]))
    for copy in copies:
        copy.wait()


def fetch(source, target, sem):
    copy = pltpu.make_async_copy(source, target, sem)
    copy.start()
    return copy


def quarter_of(index, size):
    return pl.ds(pl.multiple_of(index * size, size), size)


def forward_kernel(
    rows_ref,
    inner_ref,
    outer_in,
    outs_out,
    hidden_out,
    slope_out,
    outer_ref,
    outs_ref,
    hidden_ref,
    slope_ref,
    pre_ref,
    sems,
):
    parts, slots, quarter = rows_ref.shape
    piece = [slice(q * quarter, (q + 1) * quarter) for q in range(parts)]
    outer_copy = fetch(outer_in, outer_ref, sems.at[0])
    acc = None
    for q in range(parts):
        term = jnp.dot(rows_ref[q], inner_ref[piece[q], :], preferred_element_type=jnp.float32)
        acc = term if acc is None else acc + term
    pre_ref[...] = acc
    step = 32

    def activate(i, carry):
        at = pl.ds(pl.multiple_of(i * step, step), step)
        u = pre_ref[at, :]
        square = u * u
        tangent = jnp.tanh(u * (SQRT_TWO_PI + (SQRT_TWO_PI * CUBIC) * square))
        share = 0.5 + 0.5 * tangent
        result = u * share
        hidden_ref[at, :] = result.astype(jnp.bfloat16)
        slope_ref[at, :] = (
            share
            + result
            * (1.0 - share)
            * (2.0 * SQRT_TWO_PI + (6.0 * SQRT_TWO_PI * CUBIC) * square)
        ).astype(jnp.bfloat16)
        return carry

    lax.fori_loop(0, slots // step, activate, 0)
    saves = [
        fetch(hidden_ref, hidden_out, sems.at[1]),
        fetch(slope_ref, slope_out, sems.at[2]),
    ]
    outer_copy.wait()
    for q in range(parts):
        outs_ref[q] = jnp.dot(
            hidden_ref[...], outer_ref[:, piece[q]], preferred_element_type=jnp.float32
        ).astype(jnp.bfloat16)
        saves.append(fetch(outs_ref.at[q], outs_out.at[q], sems.at[3 + q]))
    for copy in saves:
        copy.wait()


def backward_kernel(parts, me_ref, *refs):
    cot_ins, (hidden_in, slope_in, inner_in, outer_in) = refs[:parts], refs[parts : parts + 4]
    in_refs = refs[parts + 4 : 2 * parts + 4]
    (
        cot_ref,
        hidden_ref,
        slope_ref,
        inner_ref,
        outer_ref,
        back_ref,
        grad_ref,
        pre_ref,
        sems,
    ) = refs[2 * parts + 4 :]
    slots, quarter = cot_ref.shape[1:]
    width = back_ref.shape[1]
    across = (((1,), (1,)), ((), ()))
    piece = [slice(q * quarter, (q + 1) * quarter) for q in range(parts)]

    def operands(shift):
        of = quarter_of(lax.rem(me_ref[0] + parts - shift, parts), quarter)
        return (
            fetch(cot_ins[shift], cot_ref.at[shift], sems.at[2 * shift]),
            fetch(outer_in.at[:, of], outer_ref.at[:, piece[shift]], sems.at[2 * shift + 1]),
        )

    later = ((slope_in, slope_ref), (hidden_in, hidden_ref), (inner_in, inner_ref))
    first = [operands(shift) for shift in range(parts)]
    copies = []
    acc = None
    for shift in range(parts):
        for copy in first[shift]:
            copy.wait()
        if shift < len(later):
            copies.append(fetch(*later[shift], sems.at[2 * parts + shift]))
        term = lax.dot_general(
            cot_ref[shift],
            outer_ref[:, piece[shift]],
            across,
            preferred_element_type=jnp.float32,
        )
        acc = term if acc is None else acc + term
    back_ref[...] = acc
    copies[0].wait()
    copies[1].wait()
    step = 16

    def activate(i, carry):
        at = pl.ds(pl.multiple_of(i * step, step), step)
        back = back_ref[at, :]
        pre_ref[at, :] = (back * slope_ref[at, :].astype(jnp.float32)).astype(jnp.bfloat16)
        product = back * hidden_ref[at, :].astype(jnp.float32)
        folded = product[:, :128]
        for j in range(1, width // 128):
            folded = folded + product[:, j * 128 : (j + 1) * 128]
        grad_ref[at, :] = folded
        return carry

    lax.fori_loop(0, slots // step, activate, 0)
    copies[2].wait()
    for shift in range(parts):
        of = quarter_of(lax.rem(me_ref[0] + shift, parts), quarter)
        in_refs[shift][:slots, :] = lax.dot_general(
            pre_ref[...], inner_ref[of, :], across, preferred_element_type=jnp.float32
        ).astype(jnp.bfloat16)
    gate = lax.dot_general(
        jnp.ones((8, 128), jnp.float32),
        grad_ref[...],
        across,
        precision=lax.Precision.HIGHEST,
        preferred_element_type=jnp.float32,
    )[:1, :]
    high = gate.astype(jnp.bfloat16).astype(jnp.float32)
    low = gate - high
    place = iota((EXTRA, quarter), 0)
    extra = jnp.zeros((EXTRA, quarter), jnp.float32)
    for j in range(slots // quarter):
        extra = jnp.where(place == 2 * j, high[:, piece[j]], extra)
        extra = jnp.where(place == 2 * j + 1, low[:, piece[j]], extra)
    for shift in range(parts):
        in_refs[shift][slots:, :] = extra.astype(jnp.bfloat16)


def in_pairs(terms):
    wide = [t.astype(jnp.float32) for t in terms]
    half = len(wide) // 2
    if half == 0:
        return wide[0]
    return in_pairs([wide[i] + wide[i + half] for i in range(half)])


def add_outs_kernel(outs_ref, sum_ref):
    sum_ref[...] = in_pairs([outs_ref[q] for q in range(outs_ref.shape[0])]).astype(jnp.bfloat16)


def add_kernel(out_ref, *refs):
    in_refs, sum_ref = refs[:-1], refs[-1]
    slots, quarter = out_ref.shape
    step = 16

    def add(i, carry):
        at = pl.ds(pl.multiple_of(i * step, step), step)
        sum_ref[at, :quarter] = out_ref[at, :]
        sum_ref[at, quarter : 2 * quarter] = in_pairs([ref[at, :] for ref in in_refs]).astype(
            jnp.bfloat16
        )
        return carry

    lax.fori_loop(0, slots // step, add, 0)
    chunks = slots // quarter
    split = [ref[slots:, :].astype(jnp.float32) for ref in in_refs]
    extra = [
        in_pairs([part[2 * j : 2 * j + 1, :] + part[2 * j + 1 : 2 * j + 2, :] for part in split])
        for j in range(chunks)
    ]
    lane = iota((128, 128), 1)
    for j in range(slots // 128):
        at, lanes = divmod(j * 128, quarter)
        gate = column_of(extra[at][:, lanes : lanes + 128])
        high = gate.astype(jnp.bfloat16).astype(jnp.float32)
        low = gate - high
        sum_ref[j * 128 : (j + 1) * 128, 2 * quarter :] = jnp.where(
            lane == 0, high, jnp.where(lane == 1, low, 0.0)
        ).astype(jnp.bfloat16)


def table_kernel(experts, capacity, k, ids_ref, table_ref):
    rows = ids_ref.shape[1]
    position = slot_positions(ids_ref[...], experts, capacity)[k]
    hit = iota((rows, experts * capacity), 1) == column_of(position)
    table_ref[...] = jnp.where(hit, 1.0, 0.0).astype(jnp.bfloat16)


def combine_kernel(*refs):
    table_refs, gates_ref, back_ref = refs[:TOP], refs[TOP], refs[TOP + 1]
    out_ref, in_ref, gate_ref = refs[TOP + 2 :]
    quarter = out_ref.shape[1]
    total = None
    for k in range(TOP):
        picked = jnp.dot(table_refs[k][...], back_ref[...], preferred_element_type=jnp.float32)
        term = column_of(gates_ref[k : k + 1, :]) * picked[:, : 2 * quarter]
        total = term if total is None else total + term
        gate = picked[:, 2 * quarter : 2 * quarter + 1] + picked[:, 2 * quarter + 1 : 2 * quarter + 2]
        gate_ref[k : k + 1, :] = row_of(gate)
    out_ref[...] = total[:, :quarter].astype(jnp.bfloat16)
    in_ref[...] = total[:, quarter:].astype(jnp.bfloat16)


def shift_by(x, axis, shift):
    peers = lax.axis_size(axis)
    return lax.ppermute(x, axis, [(i, (i + shift) % peers) for i in range(peers)])


def sent_on(pieces, axis):
    moved = [pieces[0]]
    for shift in range(1, len(pieces)):
        moved.append(shift_by(pieces[shift], axis, shift))
    return moved


def shape_of(shape, dtype):
    return jax.ShapeDtypeStruct(shape, dtype)


def in_hbm(x):
    return pltpu.with_memory_space_constraint(x, pltpu.HBM)


def exchange(tokens, cotangent, expert_ids, gate_values, inner_weight, outer_weight):
    rows, quarter = tokens.shape
    peers = lax.axis_size("expert")
    experts = peers * inner_weight.shape[0]
    capacity = 2 * rows * TOP // experts
    slots = experts * capacity
    parts = lax.axis_size("rep")
    inner, outer = inner_weight[0], outer_weight[0]
    depth, width = inner.shape
    ids, gates = expert_ids.T, gate_values.T
    any_spec = pl.BlockSpec(memory_space=pltpu.HBM)
    vmem_spec = pl.BlockSpec(memory_space=pltpu.VMEM)
    half, full = jnp.bfloat16, jnp.float32

    packed = pl.pallas_call(
        lambda *refs: pack_kernel(experts, capacity, *refs),
        out_shape=shape_of((slots, 2 * quarter), half),
        in_specs=[any_spec] * 3,
        scratch_shapes=[
            pltpu.VMEM(ids.shape, ids.dtype),
            pltpu.VMEM(tokens.shape, tokens.dtype),
            pltpu.VMEM(cotangent.shape, cotangent.dtype),
            pltpu.SemaphoreType.DMA((3,)),
        ],
        compiler_params=PARAMS,
        name="pack",
    )(in_hbm(ids), in_hbm(tokens), in_hbm(cotangent))
    arrived = lax.all_to_all(
        packed.reshape(peers, -1, 2 * quarter), "expert", 0, 0, tiled=True
    ).reshape(slots, 2 * quarter)
    copied, cots = pl.pallas_call(
        spread_kernel,
        out_shape=(pltpu.HBM((parts, slots, quarter), half), pltpu.HBM((slots, quarter), half)),
        in_specs=[vmem_spec],
        out_specs=(any_spec, any_spec),
        scratch_shapes=[pltpu.SemaphoreType.DMA((parts + 1,))],
        compiler_params=PARAMS,
        name="spread",
    )(arrived)
    all_rows = lax.all_to_all(copied, "rep", 0, 0, tiled=True)
    all_cots = sent_on([cots] * parts, "rep")
    tables = []
    for k in range(TOP):
        tables.append(
            pl.pallas_call(
                lambda *refs: table_kernel(experts, capacity, k, *refs),
                out_shape=shape_of((rows, slots), half),
                compiler_params=PARAMS,
            )(ids)
        )
    me = lax.axis_index("rep").astype(jnp.int32).reshape(1)
    smem_spec = pl.BlockSpec(memory_space=pltpu.SMEM)

    outs, hidden, slope = pl.pallas_call(
        forward_kernel,
        out_shape=(
            pltpu.HBM((parts, slots, quarter), half),
            pltpu.HBM((slots, width), half),
            pltpu.HBM((slots, width), half),
        ),
        in_specs=[vmem_spec, vmem_spec, any_spec],
        out_specs=(any_spec,) * 3,
        scratch_shapes=[
            pltpu.VMEM((width, depth), half),
            pltpu.VMEM((parts, slots, quarter), half),
            pltpu.VMEM((slots, width), half),
            pltpu.VMEM((slots, width), half),
            pltpu.VMEM((slots, width), full),
            pltpu.SemaphoreType.DMA((parts + 3,)),
        ],
        compiler_params=PARAMS,
        name="forward",
    )(all_rows, inner, in_hbm(outer))
    outs = lax.all_to_all(outs, "rep", 0, 0, tiled=True)
    ins = pl.pallas_call(
        lambda *refs: backward_kernel(parts, *refs),
        out_shape=(shape_of((slots + EXTRA, quarter), half),) * parts,
        in_specs=[smem_spec] + [any_spec] * (parts + 4),
        out_specs=(vmem_spec,) * parts,
        scratch_shapes=[
            pltpu.VMEM((parts, slots, quarter), half),
            pltpu.VMEM((slots, width), half),
            pltpu.VMEM((slots, width), half),
            pltpu.VMEM((depth, width), half),
            pltpu.VMEM((width, depth), half),
            pltpu.VMEM((slots, width), full),
            pltpu.VMEM((slots, 128), full),
            pltpu.VMEM((slots, width), half),
            pltpu.SemaphoreType.DMA((2 * parts + 3,)),
        ],
        compiler_params=PARAMS,
        name="backward",
    )(me, *all_cots, *[in_hbm(x) for x in (hidden, slope, inner, outer)])
    arrivals = sent_on(ins, "rep")
    out = pl.pallas_call(
        add_outs_kernel,
        out_shape=shape_of((slots, quarter), half),
        compiler_params=PARAMS,
        name="add_outs",
    )(outs)
    summed = pl.pallas_call(
        add_kernel,
        out_shape=shape_of((slots, 2 * quarter + 128), half),
        compiler_params=PARAMS,
        name="add",
    )(out, *arrivals)
    back = lax.all_to_all(
        summed.reshape(peers, -1, 2 * quarter + 128), "expert", 0, 0, tiled=True
    ).reshape(slots, 2 * quarter + 128)
    output, input_grads, gate_grads = pl.pallas_call(
        combine_kernel,
        out_shape=(
            shape_of((rows, quarter), half),
            shape_of((rows, quarter), half),
            shape_of((TOP, rows), full),
        ),
        compiler_params=PARAMS,
        name="combine",
    )(*tables, gates, back)
    return output, input_grads, gate_grads.T


def solution(mesh):
    placed = (
        P("expert", "rep"),
        P("expert", "rep"),
        P("expert", None),
        P("expert", None),
        P("expert", None, "rep"),
        P("expert", "rep", None),
    )
    return jax.shard_map(
        exchange,
        mesh=mesh,
        in_specs=placed,
        out_specs=(P("expert", "rep"), P("expert", "rep"), P("expert", None)),
        check_vma=False,
    )
```

```python
import jax
import jax.numpy as jnp
from jax import lax
from jax.experimental import pallas as pl
from jax.experimental.pallas import tpu as pltpu
from jax.sharding import PartitionSpec as P

TOP = 2
EXTRA = 16

SQRT_TWO_PI = 0.7978845608028654
CUBIC = 0.044715

PARAMS = pltpu.CompilerParams(vmem_limit_bytes=24 * 1024 * 1024)


def iota(shape, dim):
    return lax.broadcasted_iota(jnp.int32, shape, dim)


def slot_positions(ids, experts, capacity):
    rows = ids.shape[1]
    of_expert = iota((experts, rows), 0)
    named = [of_expert == ids[k : k + 1, :] for k in range(TOP)]
    both = sum(jnp.where(m, 1.0, 0.0) for m in named)
    earlier = jnp.where(iota((rows, rows), 0) < iota((rows, rows), 1), 1.0, 0.0)
    before = jnp.dot(
        both.astype(jnp.bfloat16), earlier.astype(jnp.bfloat16), preferred_element_type=jnp.float32
    )
    ranks = [jnp.sum(jnp.where(m, before, 0.0), axis=0, keepdims=True) for m in named]
    return [ids[k : k + 1, :] * capacity + ranks[k].astype(jnp.int32) for k in range(TOP)]


def column_of(row):
    n = row.shape[1]
    eye = iota((n, n), 0) == iota((n, n), 1)
    return jnp.sum(jnp.where(eye, row, jnp.zeros_like(row)), axis=1, keepdims=True)


def row_of(column):
    n = column.shape[0]
    eye = iota((n, n), 0) == iota((n, n), 1)
    return jnp.sum(jnp.where(eye, column, jnp.zeros_like(column)), axis=0, keepdims=True)


def pack_kernel(
    experts, capacity, ids_in, token_in, cot_in, out_ref, ids_ref, token_ref, cot_ref, sems
):
    copies = [
        pltpu.make_async_copy(src, dst, sems.at[i])
        for i, (src, dst) in enumerate(
            ((ids_in, ids_ref), (token_in, token_ref), (cot_in, cot_ref))
        )
    ]
    for copy in copies:
        copy.start()
    copies[0].wait()
    quarter = token_ref.shape[1]
    positions = slot_positions(ids_ref[...], experts, capacity)
    slot = iota((experts * capacity, token_ref.shape[0]), 0)
    hit = slot == positions[0]
    for k in range(1, TOP):
        hit = hit | (slot == positions[k])
    table = jnp.where(hit, 1.0, 0.0).astype(jnp.bfloat16)
    for part, ref in enumerate((token_ref, cot_ref)):
        copies[1 + part].wait()
        out_ref[:, part * quarter : (part + 1) * quarter] = jnp.dot(
            table, ref[...], preferred_element_type=jnp.float32
        ).astype(jnp.bfloat16)


def spread_kernel(arrived_ref, rows_out, cots_ref, sems):
    parts, _, quarter = rows_out.shape
    copies = [
        fetch(arrived_ref.at[:, :quarter], rows_out.at[q], sems.at[q]) for q in range(parts)
    ]
    cots_ref[...] = arrived_ref[:, quarter:]
    for copy in copies:
        copy.wait()


def fetch(source, target, sem):
    copy = pltpu.make_async_copy(source, target, sem)
    copy.start()
    return copy


def quarter_of(index, size):
    return pl.ds(pl.multiple_of(index * size, size), size)


def forward_kernel(
    rows_ref,
    inner_ref,
    outer_in,
    outs_out,
    hidden_out,
    slope_out,
    outer_ref,
    outs_ref,
    hidden_ref,
    slope_ref,
    pre_ref,
    sems,
):
    parts, slots, quarter = rows_ref.shape
    piece = [slice(q * quarter, (q + 1) * quarter) for q in range(parts)]
    outer_copy = fetch(outer_in, outer_ref, sems.at[0])
    acc = None
    for q in range(parts):
        term = jnp.dot(rows_ref[q], inner_ref[piece[q], :], preferred_element_type=jnp.float32)
        acc = term if acc is None else acc + term
    pre_ref[...] = acc
    step = 32

    def activate(i, carry):
        at = pl.ds(pl.multiple_of(i * step, step), step)
        u = pre_ref[at, :]
        square = u * u
        tangent = jnp.tanh(u * (SQRT_TWO_PI + (SQRT_TWO_PI * CUBIC) * square))
        share = 0.5 + 0.5 * tangent
        result = u * share
        hidden_ref[at, :] = result.astype(jnp.bfloat16)
        slope_ref[at, :] = (
            share
            + result
            * (1.0 - share)
            * (2.0 * SQRT_TWO_PI + (6.0 * SQRT_TWO_PI * CUBIC) * square)
        ).astype(jnp.bfloat16)
        return carry

    lax.fori_loop(0, slots // step, activate, 0)
    saves = [
        fetch(hidden_ref, hidden_out, sems.at[1]),
        fetch(slope_ref, slope_out, sems.at[2]),
    ]
    outer_copy.wait()
    for q in range(parts):
        outs_ref[q] = jnp.dot(
            hidden_ref[...], outer_ref[:, piece[q]], preferred_element_type=jnp.float32
        ).astype(jnp.bfloat16)
        saves.append(fetch(outs_ref.at[q], outs_out.at[q], sems.at[3 + q]))
    for copy in saves:
        copy.wait()


def backward_kernel(parts, me_ref, *refs):
    cot_ins, (hidden_in, slope_in, inner_in, outer_in) = refs[:parts], refs[parts : parts + 4]
    in_refs = refs[parts + 4 : 2 * parts + 4]
    (
        cot_ref,
        hidden_ref,
        slope_ref,
        inner_ref,
        outer_ref,
        back_ref,
        grad_ref,
        pre_ref,
        sems,
    ) = refs[2 * parts + 4 :]
    slots, quarter = cot_ref.shape[1:]
    width = back_ref.shape[1]
    across = (((1,), (1,)), ((), ()))
    piece = [slice(q * quarter, (q + 1) * quarter) for q in range(parts)]

    def operands(shift):
        of = quarter_of(lax.rem(me_ref[0] + parts - shift, parts), quarter)
        return (
            fetch(cot_ins[shift], cot_ref.at[shift], sems.at[2 * shift]),
            fetch(outer_in.at[:, of], outer_ref.at[:, piece[shift]], sems.at[2 * shift + 1]),
        )

    later = ((slope_in, slope_ref), (hidden_in, hidden_ref), (inner_in, inner_ref))
    first = [operands(shift) for shift in range(parts)]
    copies = []
    acc = None
    for shift in range(parts):
        for copy in first[shift]:
            copy.wait()
        if shift < len(later):
            copies.append(fetch(*later[shift], sems.at[2 * parts + shift]))
        term = lax.dot_general(
            cot_ref[shift],
            outer_ref[:, piece[shift]],
            across,
            preferred_element_type=jnp.float32,
        )
        acc = term if acc is None else acc + term
    back_ref[...] = acc
    copies[0].wait()
    copies[1].wait()
    step = 16

    def activate(i, carry):
        at = pl.ds(pl.multiple_of(i * step, step), step)
        back = back_ref[at, :]
        pre_ref[at, :] = (back * slope_ref[at, :].astype(jnp.float32)).astype(jnp.bfloat16)
        product = back * hidden_ref[at, :].astype(jnp.float32)
        folded = product[:, :128]
        for j in range(1, width // 128):
            folded = folded + product[:, j * 128 : (j + 1) * 128]
        grad_ref[at, :] = folded
        return carry

    lax.fori_loop(0, slots // step, activate, 0)
    copies[2].wait()
    for shift in range(parts):
        of = quarter_of(lax.rem(me_ref[0] + shift, parts), quarter)
        in_refs[shift][:slots, :] = lax.dot_general(
            pre_ref[...], inner_ref[of, :], across, preferred_element_type=jnp.float32
        ).astype(jnp.bfloat16)
    gate = lax.dot_general(
        jnp.ones((8, 128), jnp.float32),
        grad_ref[...],
        across,
        precision=lax.Precision.HIGHEST,
        preferred_element_type=jnp.float32,
    )[:1, :]
    high = gate.astype(jnp.bfloat16).astype(jnp.float32)
    low = gate - high
    place = iota((EXTRA, quarter), 0)
    extra = jnp.zeros((EXTRA, quarter), jnp.float32)
    for j in range(slots // quarter):
        extra = jnp.where(place == 2 * j, high[:, piece[j]], extra)
        extra = jnp.where(place == 2 * j + 1, low[:, piece[j]], extra)
    for shift in range(parts):
        in_refs[shift][slots:, :] = extra.astype(jnp.bfloat16)


def in_pairs(terms):
    wide = [t.astype(jnp.float32) for t in terms]
    half = len(wide) // 2
    if half == 0:
        return wide[0]
    return in_pairs([wide[i] + wide[i + half] for i in range(half)])


def add_outs_kernel(outs_ref, sum_ref):
    sum_ref[...] = in_pairs([outs_ref[q] for q in range(outs_ref.shape[0])]).astype(jnp.bfloat16)


def add_kernel(out_ref, *refs):
    in_refs, sum_ref = refs[:-1], refs[-1]
    slots, quarter = out_ref.shape
    step = 16

    def add(i, carry):
        at = pl.ds(pl.multiple_of(i * step, step), step)
        sum_ref[at, :quarter] = out_ref[at, :]
        sum_ref[at, quarter : 2 * quarter] = in_pairs([ref[at, :] for ref in in_refs]).astype(
            jnp.bfloat16
        )
        return carry

    lax.fori_loop(0, slots // step, add, 0)
    chunks = slots // quarter
    split = [ref[slots:, :].astype(jnp.float32) for ref in in_refs]
    extra = [
        in_pairs([part[2 * j : 2 * j + 1, :] + part[2 * j + 1 : 2 * j + 2, :] for part in split])
        for j in range(chunks)
    ]
    lane = iota((128, 128), 1)
    for j in range(slots // 128):
        at, lanes = divmod(j * 128, quarter)
        gate = column_of(extra[at][:, lanes : lanes + 128])
        high = gate.astype(jnp.bfloat16).astype(jnp.float32)
        low = gate - high
        sum_ref[j * 128 : (j + 1) * 128, 2 * quarter :] = jnp.where(
            lane == 0, high, jnp.where(lane == 1, low, 0.0)
        ).astype(jnp.bfloat16)


def table_kernel(experts, capacity, ids_ref, table_ref):
    rows = ids_ref.shape[1]
    positions = slot_positions(ids_ref[...], experts, capacity)
    slot = iota((rows, experts * capacity), 1)
    for k in range(TOP):
        hit = slot == column_of(positions[k])
        table_ref[k * rows : (k + 1) * rows, :] = jnp.where(hit, 1.0, 0.0).astype(jnp.bfloat16)


def gates_kernel(gates_ref, wide_ref):
    rows, lanes = gates_ref.shape[1], wide_ref.shape[1]
    for k in range(TOP):
        wide_ref[k * rows : (k + 1) * rows, :] = jnp.broadcast_to(
            column_of(gates_ref[k : k + 1, :]), (rows, lanes)
        )


def combine_kernel(table_ref, gates_ref, back_ref, out_ref, in_ref, gate_ref):
    rows, quarter = out_ref.shape
    picked = jnp.dot(table_ref[...], back_ref[...], preferred_element_type=jnp.float32)
    total = None
    for k in range(TOP):
        mine = picked[k * rows : (k + 1) * rows, :]
        term = gates_ref[k * rows : (k + 1) * rows, :] * mine[:, : 2 * quarter]
        total = term if total is None else total + term
        gate = mine[:, 2 * quarter : 2 * quarter + 1] + mine[:, 2 * quarter + 1 : 2 * quarter + 2]
        gate_ref[k : k + 1, :] = row_of(gate)
    out_ref[...] = total[:, :quarter].astype(jnp.bfloat16)
    in_ref[...] = total[:, quarter:].astype(jnp.bfloat16)


def shift_by(x, axis, shift):
    peers = lax.axis_size(axis)
    return lax.ppermute(x, axis, [(i, (i + shift) % peers) for i in range(peers)])


def sent_on(pieces, axis):
    moved = [pieces[0]]
    for shift in range(1, len(pieces)):
        moved.append(shift_by(pieces[shift], axis, shift))
    return moved


def shape_of(shape, dtype):
    return jax.ShapeDtypeStruct(shape, dtype)


def in_hbm(x):
    return pltpu.with_memory_space_constraint(x, pltpu.HBM)


def exchange(tokens, cotangent, expert_ids, gate_values, inner_weight, outer_weight):
    rows, quarter = tokens.shape
    peers = lax.axis_size("expert")
    experts = peers * inner_weight.shape[0]
    capacity = 2 * rows * TOP // experts
    slots = experts * capacity
    parts = lax.axis_size("rep")
    inner, outer = inner_weight[0], outer_weight[0]
    depth, width = inner.shape
    ids, gates = expert_ids.T, gate_values.T
    any_spec = pl.BlockSpec(memory_space=pltpu.HBM)
    vmem_spec = pl.BlockSpec(memory_space=pltpu.VMEM)
    half, full = jnp.bfloat16, jnp.float32

    packed = pl.pallas_call(
        lambda *refs: pack_kernel(experts, capacity, *refs),
        out_shape=shape_of((slots, 2 * quarter), half),
        in_specs=[any_spec] * 3,
        scratch_shapes=[
            pltpu.VMEM(ids.shape, ids.dtype),
            pltpu.VMEM(tokens.shape, tokens.dtype),
            pltpu.VMEM(cotangent.shape, cotangent.dtype),
            pltpu.SemaphoreType.DMA((3,)),
        ],
        compiler_params=PARAMS,
        name="pack",
    )(in_hbm(ids), in_hbm(tokens), in_hbm(cotangent))
    arrived = lax.all_to_all(
        packed.reshape(peers, -1, 2 * quarter), "expert", 0, 0, tiled=True
    ).reshape(slots, 2 * quarter)
    copied, cots = pl.pallas_call(
        spread_kernel,
        out_shape=(pltpu.HBM((parts, slots, quarter), half), shape_of((slots, quarter), half)),
        in_specs=[vmem_spec],
        out_specs=(any_spec, vmem_spec),
        scratch_shapes=[pltpu.SemaphoreType.DMA((parts,))],
        compiler_params=PARAMS,
        name="spread",
    )(arrived)
    all_rows = lax.all_to_all(copied, "rep", 0, 0, tiled=True)
    all_cots = sent_on([cots] * parts, "rep")
    table = pl.pallas_call(
        lambda *refs: table_kernel(experts, capacity, *refs),
        out_shape=shape_of((TOP * rows, slots), half),
        compiler_params=PARAMS,
        name="table",
    )(ids)
    wide_gates = pl.pallas_call(
        gates_kernel,
        out_shape=shape_of((TOP * rows, 2 * quarter), full),
        compiler_params=PARAMS,
        name="gates",
    )(gates)
    me = lax.axis_index("rep").astype(jnp.int32).reshape(1)
    smem_spec = pl.BlockSpec(memory_space=pltpu.SMEM)

    outs, hidden, slope = pl.pallas_call(
        forward_kernel,
        out_shape=(
            pltpu.HBM((parts, slots, quarter), half),
            pltpu.HBM((slots, width), half),
            pltpu.HBM((slots, width), half),
        ),
        in_specs=[vmem_spec, vmem_spec, any_spec],
        out_specs=(any_spec,) * 3,
        scratch_shapes=[
            pltpu.VMEM((width, depth), half),
            pltpu.VMEM((parts, slots, quarter), half),
            pltpu.VMEM((slots, width), half),
            pltpu.VMEM((slots, width), half),
            pltpu.VMEM((slots, width), full),
            pltpu.SemaphoreType.DMA((parts + 3,)),
        ],
        compiler_params=PARAMS,
        name="forward",
    )(all_rows, inner, in_hbm(outer))
    outs = lax.all_to_all(outs, "rep", 0, 0, tiled=True)
    ins = pl.pallas_call(
        lambda *refs: backward_kernel(parts, *refs),
        out_shape=(shape_of((slots + EXTRA, quarter), half),) * parts,
        in_specs=[smem_spec] + [any_spec] * (parts + 4),
        out_specs=(vmem_spec,) * parts,
        scratch_shapes=[
            pltpu.VMEM((parts, slots, quarter), half),
            pltpu.VMEM((slots, width), half),
            pltpu.VMEM((slots, width), half),
            pltpu.VMEM((depth, width), half),
            pltpu.VMEM((width, depth), half),
            pltpu.VMEM((slots, width), full),
            pltpu.VMEM((slots, 128), full),
            pltpu.VMEM((slots, width), half),
            pltpu.SemaphoreType.DMA((2 * parts + 3,)),
        ],
        compiler_params=PARAMS,
        name="backward",
    )(me, *all_cots, *[in_hbm(x) for x in (hidden, slope, inner, outer)])
    arrivals = sent_on(ins, "rep")
    out = pl.pallas_call(
        add_outs_kernel,
        out_shape=shape_of((slots, quarter), half),
        compiler_params=PARAMS,
        name="add_outs",
    )(outs)
    summed = pl.pallas_call(
        add_kernel,
        out_shape=shape_of((slots, 2 * quarter + 128), half),
        compiler_params=PARAMS,
        name="add",
    )(out, *arrivals)
    back = lax.all_to_all(
        summed.reshape(peers, -1, 2 * quarter + 128), "expert", 0, 0, tiled=True
    ).reshape(slots, 2 * quarter + 128)
    output, input_grads, gate_grads = pl.pallas_call(
        combine_kernel,
        out_shape=(
            shape_of((rows, quarter), half),
            shape_of((rows, quarter), half),
            shape_of((TOP, rows), full),
        ),
        compiler_params=PARAMS,
        name="combine",
    )(table, wide_gates, back)
    return output, input_grads, gate_grads.T


def solution(mesh):
    placed = (
        P("expert", "rep"),
        P("expert", "rep"),
        P("expert", None),
        P("expert", None),
        P("expert", None, "rep"),
        P("expert", "rep", None),
    )
    return jax.shard_map(
        exchange,
        mesh=mesh,
        in_specs=placed,
        out_specs=(P("expert", "rep"), P("expert", "rep"), P("expert", None)),
        check_vma=False,
    )
```

```python
import jax
import jax.numpy as jnp
from jax import lax
from jax.experimental import pallas as pl
from jax.experimental.pallas import tpu as pltpu
from jax.sharding import PartitionSpec as P

TOP = 2
EXTRA = 16

SQRT_TWO_PI = 0.7978845608028654
CUBIC = 0.044715

PARAMS = pltpu.CompilerParams(vmem_limit_bytes=24 * 1024 * 1024)


def iota(shape, dim):
    return lax.broadcasted_iota(jnp.int32, shape, dim)


def slot_positions(ids, experts, capacity):
    rows = ids.shape[1]
    of_expert = iota((experts, rows), 0)
    named = [of_expert == ids[k : k + 1, :] for k in range(TOP)]
    both = sum(jnp.where(m, 1.0, 0.0) for m in named)
    earlier = jnp.where(iota((rows, rows), 0) < iota((rows, rows), 1), 1.0, 0.0)
    before = jnp.dot(
        both.astype(jnp.bfloat16), earlier.astype(jnp.bfloat16), preferred_element_type=jnp.float32
    )
    ranks = [jnp.sum(jnp.where(m, before, 0.0), axis=0, keepdims=True) for m in named]
    return [ids[k : k + 1, :] * capacity + ranks[k].astype(jnp.int32) for k in range(TOP)]


def column_of(row):
    n = row.shape[1]
    eye = iota((n, n), 0) == iota((n, n), 1)
    return jnp.sum(jnp.where(eye, row, jnp.zeros_like(row)), axis=1, keepdims=True)


def row_of(column):
    n = column.shape[0]
    eye = iota((n, n), 0) == iota((n, n), 1)
    return jnp.sum(jnp.where(eye, column, jnp.zeros_like(column)), axis=0, keepdims=True)


def pack_kernel(
    experts, capacity, ids_in, token_in, cot_in, out_ref, ids_ref, token_ref, cot_ref, sems
):
    copies = [
        pltpu.make_async_copy(src, dst, sems.at[i])
        for i, (src, dst) in enumerate(
            ((ids_in, ids_ref), (token_in, token_ref), (cot_in, cot_ref))
        )
    ]
    for copy in copies:
        copy.start()
    copies[0].wait()
    quarter = token_ref.shape[1]
    positions = slot_positions(ids_ref[...], experts, capacity)
    slot = iota((experts * capacity, token_ref.shape[0]), 0)
    hit = slot == positions[0]
    for k in range(1, TOP):
        hit = hit | (slot == positions[k])
    table = jnp.where(hit, 1.0, 0.0).astype(jnp.bfloat16)
    for part, ref in enumerate((token_ref, cot_ref)):
        copies[1 + part].wait()
        out_ref[:, part * quarter : (part + 1) * quarter] = jnp.dot(
            table, ref[...], preferred_element_type=jnp.float32
        ).astype(jnp.bfloat16)


def spread_kernel(arrived_ref, rows_out, cots_out, sems):
    parts, _, quarter = rows_out.shape
    copies = [
        fetch(arrived_ref.at[:, :quarter], rows_out.at[q], sems.at[q]) for q in range(parts)
    ]
    copies.append(fetch(arrived_ref.at[:, quarter:], cots_out, sems.at[parts]))
    for copy in copies:
        copy.wait()


def fetch(source, target, sem):
    copy = pltpu.make_async_copy(source, target, sem)
    copy.start()
    return copy


def quarter_of(index, size):
    return pl.ds(pl.multiple_of(index * size, size), size)


def gelu_parts(u):
    square = u * u
    tangent = jnp.tanh(u * (SQRT_TWO_PI + (SQRT_TWO_PI * CUBIC) * square))
    share = 0.5 + 0.5 * tangent
    result = u * share
    return result, share, 2.0 * SQRT_TWO_PI + (6.0 * SQRT_TWO_PI * CUBIC) * square


def forward_kernel(
    rows_ref,
    inner_ref,
    outer_in,
    outs_out,
    save_out,
    outer_ref,
    outs_ref,
    hidden_ref,
    save_ref,
    pre_ref,
    sems,
):
    parts, slots, quarter = rows_ref.shape
    piece = [slice(q * quarter, (q + 1) * quarter) for q in range(parts)]
    outer_copy = fetch(outer_in, outer_ref, sems.at[0])
    acc = None
    for q in range(parts):
        term = jnp.dot(rows_ref[q], inner_ref[piece[q], :], preferred_element_type=jnp.float32)
        acc = term if acc is None else acc + term
    pre_ref[...] = acc
    step = 32

    def activate(i, carry):
        at = pl.ds(pl.multiple_of(i * step, step), step)
        u = pre_ref[at, :]
        hidden_ref[at, :] = gelu_parts(u)[0].astype(jnp.bfloat16)
        save_ref[at, :] = u.astype(jnp.bfloat16)
        return carry

    lax.fori_loop(0, slots // step, activate, 0)
    saves = [fetch(save_ref, save_out, sems.at[1])]
    outer_copy.wait()
    for q in range(parts):
        outs_ref[q] = jnp.dot(
            hidden_ref[...], outer_ref[:, piece[q]], preferred_element_type=jnp.float32
        ).astype(jnp.bfloat16)
        saves.append(fetch(outs_ref.at[q], outs_out.at[q], sems.at[2 + q]))
    for copy in saves:
        copy.wait()


def backward_kernel(parts, me_ref, *refs):
    cot_ins, (saved_in, inner_in, outer_in) = refs[:parts], refs[parts : parts + 3]
    in_refs = refs[parts + 3 : 2 * parts + 3]
    cot_ref, saved_ref, inner_ref, outer_ref, back_ref, grad_ref, pre_ref, sems = refs[
        2 * parts + 3 :
    ]
    slots, quarter = cot_ref.shape[1:]
    width = back_ref.shape[1]
    across = (((1,), (1,)), ((), ()))
    piece = [slice(q * quarter, (q + 1) * quarter) for q in range(parts)]

    def operands(shift):
        of = quarter_of(lax.rem(me_ref[0] + parts - shift, parts), quarter)
        return (
            fetch(cot_ins[shift], cot_ref.at[shift], sems.at[2 * shift]),
            fetch(outer_in.at[:, of], outer_ref.at[:, piece[shift]], sems.at[2 * shift + 1]),
        )

    later = ((saved_in, saved_ref), (inner_in, inner_ref))
    first = [operands(shift) for shift in range(parts)]
    copies = []
    acc = None
    for shift in range(parts):
        for copy in first[shift]:
            copy.wait()
        if shift < len(later):
            copies.append(fetch(*later[shift], sems.at[2 * parts + shift]))
        term = lax.dot_general(
            cot_ref[shift],
            outer_ref[:, piece[shift]],
            across,
            preferred_element_type=jnp.float32,
        )
        acc = term if acc is None else acc + term
    back_ref[...] = acc
    copies[0].wait()
    step = 16

    def activate(i, carry):
        at = pl.ds(pl.multiple_of(i * step, step), step)
        back = back_ref[at, :]
        result, share, factor = gelu_parts(saved_ref[at, :].astype(jnp.float32))
        slope = share + result * (1.0 - share) * factor
        pre_ref[at, :] = (back * slope).astype(jnp.bfloat16)
        product = back * result
        folded = product[:, :128]
        for j in range(1, width // 128):
            folded = folded + product[:, j * 128 : (j + 1) * 128]
        grad_ref[at, :] = folded
        return carry

    lax.fori_loop(0, slots // step, activate, 0)
    copies[1].wait()
    for shift in range(parts):
        of = quarter_of(lax.rem(me_ref[0] + shift, parts), quarter)
        in_refs[shift][:slots, :] = lax.dot_general(
            pre_ref[...], inner_ref[of, :], across, preferred_element_type=jnp.float32
        ).astype(jnp.bfloat16)
    gate = lax.dot_general(
        jnp.ones((8, 128), jnp.float32),
        grad_ref[...],
        across,
        precision=lax.Precision.HIGHEST,
        preferred_element_type=jnp.float32,
    )[:1, :]
    high = gate.astype(jnp.bfloat16).astype(jnp.float32)
    low = gate - high
    place = iota((EXTRA, quarter), 0)
    extra = jnp.zeros((EXTRA, quarter), jnp.float32)
    for j in range(slots // quarter):
        extra = jnp.where(place == 2 * j, high[:, piece[j]], extra)
        extra = jnp.where(place == 2 * j + 1, low[:, piece[j]], extra)
    for shift in range(parts):
        in_refs[shift][slots:, :] = extra.astype(jnp.bfloat16)


def in_pairs(terms):
    wide = [t.astype(jnp.float32) for t in terms]
    half = len(wide) // 2
    if half == 0:
        return wide[0]
    return in_pairs([wide[i] + wide[i + half] for i in range(half)])


def add_outs_kernel(outs_ref, sum_ref):
    sum_ref[...] = in_pairs([outs_ref[q] for q in range(outs_ref.shape[0])]).astype(jnp.bfloat16)


def add_kernel(out_ref, *refs):
    in_refs, sum_ref = refs[:-1], refs[-1]
    slots, quarter = out_ref.shape
    step = 16

    def add(i, carry):
        at = pl.ds(pl.multiple_of(i * step, step), step)
        sum_ref[at, :quarter] = out_ref[at, :]
        sum_ref[at, quarter : 2 * quarter] = in_pairs([ref[at, :] for ref in in_refs]).astype(
            jnp.bfloat16
        )
        return carry

    lax.fori_loop(0, slots // step, add, 0)
    chunks = slots // quarter
    split = [ref[slots:, :].astype(jnp.float32) for ref in in_refs]
    extra = [
        in_pairs([part[2 * j : 2 * j + 1, :] + part[2 * j + 1 : 2 * j + 2, :] for part in split])
        for j in range(chunks)
    ]
    lane = iota((128, 128), 1)
    for j in range(slots // 128):
        at, lanes = divmod(j * 128, quarter)
        gate = column_of(extra[at][:, lanes : lanes + 128])
        high = gate.astype(jnp.bfloat16).astype(jnp.float32)
        low = gate - high
        sum_ref[j * 128 : (j + 1) * 128, 2 * quarter :] = jnp.where(
            lane == 0, high, jnp.where(lane == 1, low, 0.0)
        ).astype(jnp.bfloat16)


def table_kernel(experts, capacity, k, ids_ref, table_ref):
    rows = ids_ref.shape[1]
    position = slot_positions(ids_ref[...], experts, capacity)[k]
    hit = iota((rows, experts * capacity), 1) == column_of(position)
    table_ref[...] = jnp.where(hit, 1.0, 0.0).astype(jnp.bfloat16)


def combine_kernel(*refs):
    table_refs, gates_ref, back_ref = refs[:TOP], refs[TOP], refs[TOP + 1]
    out_ref, in_ref, gate_ref = refs[TOP + 2 :]
    quarter = out_ref.shape[1]
    total = None
    for k in range(TOP):
        picked = jnp.dot(table_refs[k][...], back_ref[...], preferred_element_type=jnp.float32)
        term = column_of(gates_ref[k : k + 1, :]) * picked[:, : 2 * quarter]
        total = term if total is None else total + term
        gate = picked[:, 2 * quarter : 2 * quarter + 1] + picked[:, 2 * quarter + 1 : 2 * quarter + 2]
        gate_ref[k : k + 1, :] = row_of(gate)
    out_ref[...] = total[:, :quarter].astype(jnp.bfloat16)
    in_ref[...] = total[:, quarter:].astype(jnp.bfloat16)


def shift_by(x, axis, shift):
    peers = lax.axis_size(axis)
    return lax.ppermute(x, axis, [(i, (i + shift) % peers) for i in range(peers)])


def sent_on(pieces, axis):
    moved = [pieces[0]]
    for shift in range(1, len(pieces)):
        moved.append(shift_by(pieces[shift], axis, shift))
    return moved


def shape_of(shape, dtype):
    return jax.ShapeDtypeStruct(shape, dtype)


def in_hbm(x):
    return pltpu.with_memory_space_constraint(x, pltpu.HBM)


def exchange(tokens, cotangent, expert_ids, gate_values, inner_weight, outer_weight):
    rows, quarter = tokens.shape
    peers = lax.axis_size("expert")
    experts = peers * inner_weight.shape[0]
    capacity = 2 * rows * TOP // experts
    slots = experts * capacity
    parts = lax.axis_size("rep")
    inner, outer = inner_weight[0], outer_weight[0]
    depth, width = inner.shape
    ids, gates = expert_ids.T, gate_values.T
    any_spec = pl.BlockSpec(memory_space=pltpu.HBM)
    vmem_spec = pl.BlockSpec(memory_space=pltpu.VMEM)
    half, full = jnp.bfloat16, jnp.float32

    packed = pl.pallas_call(
        lambda *refs: pack_kernel(experts, capacity, *refs),
        out_shape=shape_of((slots, 2 * quarter), half),
        in_specs=[any_spec] * 3,
        scratch_shapes=[
            pltpu.VMEM(ids.shape, ids.dtype),
            pltpu.VMEM(tokens.shape, tokens.dtype),
            pltpu.VMEM(cotangent.shape, cotangent.dtype),
            pltpu.SemaphoreType.DMA((3,)),
        ],
        compiler_params=PARAMS,
        name="pack",
    )(in_hbm(ids), in_hbm(tokens), in_hbm(cotangent))
    arrived = lax.all_to_all(
        packed.reshape(peers, -1, 2 * quarter), "expert", 0, 0, tiled=True
    ).reshape(slots, 2 * quarter)
    copied, cots = pl.pallas_call(
        spread_kernel,
        out_shape=(pltpu.HBM((parts, slots, quarter), half), pltpu.HBM((slots, quarter), half)),
        in_specs=[vmem_spec],
        out_specs=(any_spec, any_spec),
        scratch_shapes=[pltpu.SemaphoreType.DMA((parts + 1,))],
        compiler_params=PARAMS,
        name="spread",
    )(arrived)
    all_rows = lax.all_to_all(copied, "rep", 0, 0, tiled=True)
    all_cots = sent_on([cots] * parts, "rep")
    tables = []
    for k in range(TOP):
        tables.append(
            pl.pallas_call(
                lambda *refs: table_kernel(experts, capacity, k, *refs),
                out_shape=shape_of((rows, slots), half),
                compiler_params=PARAMS,
            )(ids)
        )
    me = lax.axis_index("rep").astype(jnp.int32).reshape(1)
    smem_spec = pl.BlockSpec(memory_space=pltpu.SMEM)

    outs, saved = pl.pallas_call(
        forward_kernel,
        out_shape=(
            pltpu.HBM((parts, slots, quarter), half),
            pltpu.HBM((slots, width), half),
        ),
        in_specs=[vmem_spec, vmem_spec, any_spec],
        out_specs=(any_spec,) * 2,
        scratch_shapes=[
            pltpu.VMEM((width, depth), half),
            pltpu.VMEM((parts, slots, quarter), half),
            pltpu.VMEM((slots, width), half),
            pltpu.VMEM((slots, width), half),
            pltpu.VMEM((slots, width), full),
            pltpu.SemaphoreType.DMA((parts + 2,)),
        ],
        compiler_params=PARAMS,
        name="forward",
    )(all_rows, inner, in_hbm(outer))
    outs = lax.all_to_all(outs, "rep", 0, 0, tiled=True)
    ins = pl.pallas_call(
        lambda *refs: backward_kernel(parts, *refs),
        out_shape=(shape_of((slots + EXTRA, quarter), half),) * parts,
        in_specs=[smem_spec] + [any_spec] * (parts + 3),
        out_specs=(vmem_spec,) * parts,
        scratch_shapes=[
            pltpu.VMEM((parts, slots, quarter), half),
            pltpu.VMEM((slots, width), half),
            pltpu.VMEM((depth, width), half),
            pltpu.VMEM((width, depth), half),
            pltpu.VMEM((slots, width), full),
            pltpu.VMEM((slots, 128), full),
            pltpu.VMEM((slots, width), half),
            pltpu.SemaphoreType.DMA((2 * parts + 2,)),
        ],
        compiler_params=PARAMS,
        name="backward",
    )(me, *all_cots, *[in_hbm(x) for x in (saved, inner, outer)])
    arrivals = sent_on(ins, "rep")
    out = pl.pallas_call(
        add_outs_kernel,
        out_shape=shape_of((slots, quarter), half),
        compiler_params=PARAMS,
        name="add_outs",
    )(outs)
    summed = pl.pallas_call(
        add_kernel,
        out_shape=shape_of((slots, 2 * quarter + 128), half),
        compiler_params=PARAMS,
        name="add",
    )(out, *arrivals)
    back = lax.all_to_all(
        summed.reshape(peers, -1, 2 * quarter + 128), "expert", 0, 0, tiled=True
    ).reshape(slots, 2 * quarter + 128)
    output, input_grads, gate_grads = pl.pallas_call(
        combine_kernel,
        out_shape=(
            shape_of((rows, quarter), half),
            shape_of((rows, quarter), half),
            shape_of((TOP, rows), full),
        ),
        compiler_params=PARAMS,
        name="combine",
    )(*tables, gates, back)
    return output, input_grads, gate_grads.T


def solution(mesh):
    placed = (
        P("expert", "rep"),
        P("expert", "rep"),
        P("expert", None),
        P("expert", None),
        P("expert", None, "rep"),
        P("expert", "rep", None),
    )
    return jax.shard_map(
        exchange,
        mesh=mesh,
        in_specs=placed,
        out_specs=(P("expert", "rep"), P("expert", "rep"), P("expert", None)),
        check_vma=False,
    )
```
